128 devices in a mesh: aux: 8 (over x, core), pair: 16 (over y, z).
Axes of the slice: x: 4, y: 4, z: 4, core: 2. Of those that a mesh axis runs over, the one named last changes fastest.
Arguments:
- three_centre: bfloat16 [96, 64, 128, 128], P('aux', 'pair'), may hold values from -6 to 6
- occ_green: bfloat16 [2048, 2048], P('pair'), as said below
- virt_green: bfloat16 [2048, 2048], replicated, may hold values from -0.25 to 0.25
- tile_cols: int32 [16, 4], replicated, may hold values from 0 to 15, as said below
- tile_live: int32 [16], replicated, may hold values from 1 to 4, as said below
Outputs:
- polarizability: float32 [96, 96], P('pair', 'aux')
The draws below stay inside these ranges and needn't reach their ends.
Inputs may be any that keep to these rules, and one draw needn't show every extreme that they name: occ_green is symmetric. `tile_cols`: the 4 column blocks of one block row are distinct. `tile_live`: some block row has all 4 slots live.
All inputs are finite; a program needn't handle non-finite values.
Results may differ from the reference program's by a relative error of at most 0.015.
Values may be sent and summed in bfloat16 or wider, within the bound.
A program may use at most 192 MiB of HBM per device.

```python
import math
import jax
import jax.numpy as jnp
from jax import lax

TB = 128
TILE = 4
NBLK = 16
NB = 2048
NT = 64
NAUX = 96
N_PAIR = 16


def draw_occ_green(key, part):
    base = jax.random.normal(key, (NB, NB), jnp.float32)
    return ((base + base.T) * (0.5 / NB) ** 0.5).astype(jnp.bfloat16)


def draw_tile_cols(key, part):
    row_keys = jax.random.split(key, NBLK)
    picked = jax.vmap(lambda single: jax.random.permutation(single, NBLK)[:TILE])(row_keys)
    return picked.astype(jnp.int32)


def draw_tile_live(key, part):
    counts = jax.random.randint(key, (NBLK,), 1, TILE + 1)
    fullest = jax.random.randint(jax.random.fold_in(key, 3), (), 0, NBLK)
    return jnp.where(jnp.arange(NBLK) == fullest, TILE, counts).astype(jnp.int32)


def block_scale(key, extent, shards, least, top_value):
    def one(position, blocks):
        heights = jax.random.uniform(jax.random.fold_in(jax.random.fold_in(key, 6), position), (blocks,), jnp.float32, least / len(shards), top_value / len(shards))
        return jnp.repeat(jnp.exp(heights), extent[position] // blocks).reshape((-1,) + (1,) * (len(extent) - position - 1))

    level = one(*shards[0])
    for cut in shards[1:]:
        level = level * one(*cut)
    return level


def noise(stream_key, shape, width, limit, shards=(), kind=jnp.bfloat16):
    level = block_scale(stream_key, shape, shards, -0.22, 0.18) if shards else 1.0
    values = jax.random.normal(stream_key, shape, jnp.float32) * width * level
    return jnp.minimum(jnp.maximum(values, -limit), limit).astype(kind)


def setup_inputs(seed: int = 0) -> dict:
    seeds = jax.random.split(jax.random.key(seed), 6)
    three_centre = noise(seeds[0], (NAUX, NT, TB, TB), 1.0, 6.0, ((0, 8), (1, 16)))
    occ_green = draw_occ_green(jax.random.fold_in(seeds[5], 71), 0)
    virt_green = noise(seeds[2], (NB, NB), (TB * TILE) ** -0.5, 0.25)
    tile_cols = draw_tile_cols(jax.random.fold_in(seeds[5], 71), 0)
    tile_live = draw_tile_live(jax.random.fold_in(seeds[5], 71), 0)
    return {"three_centre": three_centre, "occ_green": occ_green, "virt_green": virt_green, "tile_cols": tile_cols, "tile_live": tile_live}


def reference(three_centre, occ_green, virt_green, tile_cols, tile_live):
    slot_index = jnp.arange(TILE, dtype=jnp.int32)
    live_rows = (slot_index[None, :] < tile_live[:, None]).astype(jnp.float32)
    flat_cols = tile_cols.reshape(NT).astype(jnp.int32)
    virt_rows = jnp.take(virt_green.reshape(N_PAIR, TB, NB), flat_cols, axis=0)
    virt_rows = virt_rows.astype(jnp.float32).reshape(N_PAIR, TILE, TB, N_PAIR, TB)
    occ_blocks = occ_green.astype(jnp.float32).reshape(N_PAIR, TB, N_PAIR, TB)

    def one_row(tiles):
        blocks = tiles.astype(jnp.float32).reshape(N_PAIR, TILE, TB, TB) * live_rows[:, :, None, None]
        half = jnp.einsum('ksab,ksbjc->kajc', blocks, virt_rows)
        half = lax.optimization_barrier(half.astype(jnp.bfloat16)).astype(jnp.float32)
        picked = jnp.take(half, flat_cols, axis=2)
        picked = picked.reshape(N_PAIR, TB, N_PAIR, TILE, TB)
        terms = jnp.einsum('iakb,kbisc->kisac', occ_blocks, picked)
        terms = lax.optimization_barrier(terms.astype(jnp.bfloat16)).astype(jnp.float32)
        polar = lax.optimization_barrier(jnp.sum(terms, axis=0))
        return polar.astype(jnp.bfloat16).reshape(NT * TB * TB)
    polar_tiles = lax.map(one_row, three_centre)
    live_flat = live_rows.reshape(NT).astype(jnp.bfloat16)
    masked = (three_centre * live_flat[None, :, None, None]).reshape(NAUX, NT * TB * TB)
    chi = lax.dot_general(masked, polar_tiles, (((1,), (1,)), ((), ())), preferred_element_type=jnp.float32)
    return chi * (1.0 / (TB * math.sqrt(NT)))
```

```python
import functools
import math

import jax
import jax.numpy as jnp
from jax import lax
from jax.experimental import pallas as pl
from jax.experimental.pallas import tpu as pltpu
from jax.sharding import PartitionSpec as P

MESH = pl.DeviceIdType.MESH
F32 = jnp.float32
BF16 = jnp.bfloat16
UNITS = (
    (0, 0), (1, 0), (0, 1), (0, 3), (0, 2), (2, 0),
    (1, 1), (1, 3), (1, 2), (2, 1), (2, 3), (2, 2),
)


def kernel(
    factor,
    cols_ref, live_ref, t_ref, o_ref, v_ref, out_ref,
    tq0, tq1, tq2, orow, vv, tp, nn, dd, xs, xr, part, red,
    loc, zs, zr, hs, hr, ps, pr, ysr, yrr, ysl, yrl, fsr, frr, fsl, frl,
    asr, arr, asl, arl, gs, gr, cs, cr, es, er, rs, rr,
):
    tqs = (tq0, tq1, tq2)
    g = lax.axis_index("aux")
    k = lax.axis_index("pair")
    y, z = k // 4, k % 4
    x, core = g // 2, g % 2
    partner = x * 2 + 1 - core
    g_right, g_left, g_far = (
        ((x + 1) % 4) * 2 + core, ((x + 3) % 4) * 2 + core, ((x + 2) % 4) * 2 + core,
    )
    y_right, y_left, y_far = (y + 1) % 4, (y + 3) % 4, (y + 2) % 4
    k_right, k_left = y_right * 4 + z, y_left * 4 + z
    here = (g, k)

    barrier = pltpu.get_barrier_semaphore()
    peers = [(g, (k + d) % 16) for d in range(1, 16)]
    peers += [(g_right, k), (g_left, k), (partner, k)]
    for peer in peers:
        pl.semaphore_signal(barrier, inc=1, device_id=peer, device_id_type=MESH)

    def tiles(q, row, first=0, count=4):
        return tqs[q].at[pl.ds(4 * row + first, count)]

    started = []

    def local(src, dst, sem):
        copy = pltpu.make_async_copy(src, dst, sem)
        copy.start()
        return copy

    def send(src, dst, send_sem, recv_sem, device):
        copy = pltpu.make_async_remote_copy(
            src_ref=src, dst_ref=dst, send_sem=send_sem, recv_sem=recv_sem,
            device_id=device, device_id_type=MESH,
        )
        copy.start()
        started.append(copy)

    def arrived(dst, send_sem, recv_sem):
        pltpu.make_async_remote_copy(
            src_ref=dst, dst_ref=dst, send_sem=send_sem, recv_sem=recv_sem,
            device_id=(partner, k), device_id_type=MESH,
        ).wait_recv()

    locals_ = [local(t_ref.at[3 * z + q], tiles(q, k), loc.at[q]) for q in range(3)]
    locals_.append(local(t_ref, tp.at[g], loc.at[3]))
    locals_.append(local(o_ref, orow.at[pl.ds(pl.multiple_of(128 * z, 128), 128)], loc.at[4]))
    for c in range(16):
        locals_.append(local(v_ref.at[:, pl.ds(128 * c, 128)], vv.at[c], loc.at[5 + c]))
    pl.semaphore_wait(barrier, len(peers))

    def z_sends(q):
        for dz in (1, 3, 2):
            to = (z + dz) % 4
            send(
                t_ref.at[3 * to + q], tiles(q, k), zs.at[q, dz - 1], zr.at[q, dz - 1],
                (g, y * 4 + to),
            )

    def slot(row, dz):
        return row * 4 + (z + 4 - dz) % 4

    def inject(q, dz):
        at = slot(y, dz)
        if dz:
            arrived(tiles(q, at), zs.at[q, dz - 1], zr.at[q, dz - 1])
        src = tiles(q, at) if dz else t_ref.at[3 * z + q]
        send(src, tiles(q, at), ysr.at[q, dz], yrr.at[q, dz], (g, k_right))
        send(src, tiles(q, at), ysl.at[q, dz], yrl.at[q, dz], (g, k_left))

    def relay(q, dz):
        from_left, from_right = slot(y_left, dz), slot(y_right, dz)
        arrived(tiles(q, from_left), ysr.at[q, dz], yrr.at[q, dz])
        half = tiles(q, from_left, 0, 2)
        send(half, half, fsr.at[q, dz], frr.at[q, dz], (g, k_right))
        arrived(tiles(q, from_right), ysl.at[q, dz], yrl.at[q, dz])
        half = tiles(q, from_right, 2, 2)
        send(half, half, fsl.at[q, dz], frl.at[q, dz], (g, k_left))

    def far(q, dz):
        at = slot(y_far, dz)
        arrived(tiles(q, at, 0, 2), fsr.at[q, dz], frr.at[q, dz])
        arrived(tiles(q, at, 2, 2), fsl.at[q, dz], frl.at[q, dz])

    half_rows = pl.multiple_of(64 * core, 64)

    def o_sends():
        for dz in (1, 3, 2):
            to = (z + dz) % 4
            at = orow.at[pl.ds(pl.multiple_of(128 * z + half_rows, 64), 64)]
            send(
                o_ref.at[pl.ds(half_rows, 64)], at, hs.at[dz - 1], hr.at[dz - 1],
                (g, y * 4 + to),
            )

    def o_share():
        for dz in (1, 3, 2):
            row = pl.multiple_of(128 * ((z + 4 - dz) % 4) + half_rows, 64)
            at = orow.at[pl.ds(row, 64)]
            arrived(at, hs.at[dz - 1], hr.at[dz - 1])
            send(at, at, ps.at[dz - 1], pr.at[dz - 1], (partner, k))

    def o_done():
        for dz in (1, 3, 2):
            row = pl.multiple_of(128 * ((z + 4 - dz) % 4) + 64 - half_rows, 64)
            arrived(orow.at[pl.ds(row, 64)], ps.at[dz - 1], pr.at[dz - 1])

    def chunk(owner, j):
        return tp.at[owner, pl.ds(3 * j, 3)]

    def x_sends(j):
        src = t_ref.at[pl.ds(3 * j, 3)]
        send(src, chunk(g, j), asr.at[j], arr.at[j], (g_right, k))
        send(src, chunk(g, j), asl.at[j], arl.at[j], (g_left, k))
        send(src, chunk(g, j), cs.at[0, j], cr.at[0, j], (partner, k))

    def x_relay(j):
        at = chunk(g_left, j)
        arrived(at, asr.at[j], arr.at[j])
        if j < 2:
            send(at, at, gs.at[j], gr.at[j], (g_right, k))
        send(at, at, cs.at[1, j], cr.at[1, j], (partner, k))
        at = chunk(g_right, j)
        arrived(at, asl.at[j], arl.at[j])
        if j >= 2:
            send(at, at, gs.at[j], gr.at[j], (g_left, k))
        send(at, at, cs.at[2, j], cr.at[2, j], (partner, k))

    def x_far(j):
        at = chunk(g_far, j)
        arrived(at, gs.at[j], gr.at[j])
        send(at, at, cs.at[3, j], cr.at[3, j], (partner, k))

    def x_done(j):
        other = 1 - core
        for n, dx in enumerate((0, 3, 1, 2)):
            owner = ((x + dx) % 4) * 2 + other
            arrived(chunk(owner, j), cs.at[n, j], cr.at[n, j])

    z_sends(0)
    inject(*UNITS[0])
    x_sends(0)
    inject(*UNITS[1])
    o_sends()
    z_sends(1)
    z_sends(2)
    for j in range(1, 4):
        x_sends(j)
    for n in range(2, 12):
        inject(*UNITS[n])
        relay(*UNITS[n - 2])
        if n == 4:
            o_share()
        if n in (3, 5, 7, 9):
            x_relay((n - 3) // 2)
    relay(*UNITS[10])
    relay(*UNITS[11])
    for j in range(4):
        x_far(j)
    o_done()
    for copy in locals_:
        copy.wait()
    for unit in UNITS:
        far(*unit)

    for q in range(3):
        tq = tqs[q]

        def columns(pair, carry):
            for h in range(2):
                c = 2 * pair + h
                for i in range(16):
                    c0, c1, c2, c3 = (cols_ref[i, s] for s in range(4))
                    s = jnp.where(c1 == c, 1, jnp.where(c2 == c, 2, jnp.where(c3 == c, 3, 0)))
                    hit = (c0 == c) | (c1 == c) | (c2 == c) | (c3 == c)
                    keep = hit & (s < live_ref[i])
                    tile = tq[4 * i + s]
                    dd[pl.ds(128 * i, 128), pl.ds(128 * h, 128)] = jnp.where(
                        keep, tile, jnp.zeros_like(tile)
                    )
            acc = jnp.dot(orow[...], dd[...], preferred_element_type=F32)
            nn[:, pl.ds(pl.multiple_of(256 * pair, 256), 256)] = acc.astype(BF16)
            return carry

        lax.fori_loop(0, 8, columns, 0)

        def rows(r, carry):
            lhs = nn[pl.ds(pl.multiple_of(128 * r, 128), 128), :]
            for s in range(0, 4, 2):
                rhs = jnp.concatenate([vv[cols_ref[y * 4 + r, s + e]] for e in range(2)], axis=1)
                acc = jnp.dot(lhs, rhs, preferred_element_type=F32).astype(BF16)
                xs[q, r, s] = acc[:, :128]
                xs[q, r, s + 1] = acc[:, 128:]
            return carry

        lax.fori_loop(0, 4, rows, 0)

    for q in range(3):
        for dz in (1, 3, 2):
            to = (z + dz) % 4
            send(
                xs.at[q, to], xr.at[3 * z + q], es.at[q, dz - 1], er.at[q, dz - 1],
                (g, y * 4 + to),
            )
    own = [local(xs.at[q, z], xr.at[3 * z + q], loc.at[q]) for q in range(3)]
    for j in range(4):
        x_done(j)
    for q in range(3):
        for dz in (1, 3, 2):
            at = xr.at[3 * ((z + 4 - dz) % 4) + q]
            arrived(at, es.at[q, dz - 1], er.at[q, dz - 1])
    for copy in own:
        copy.wait()

    mine = live_ref[k]
    for s in range(4):
        xr[:, s] = jnp.where(s < mine, xr[:, s], jnp.zeros_like(xr[:, s]))
    row = lax.broadcasted_iota(jnp.int32, (192, 192), 0)
    col = lax.broadcasted_iota(jnp.int32, (192, 192), 1)
    same = (row % 16) == (col % 16)
    pick = (
        lax.broadcasted_iota(jnp.int32, (192, 128), 0) // 16
        == lax.broadcasted_iota(jnp.int32, (192, 128), 1)
    ).astype(F32)

    def contract(owner, carry):
        acc = jnp.zeros((192, 192), F32)
        for s in range(0, 4, 2):
            for a in range(0, 128, 16):
                lhs = jnp.concatenate(
                    [tp[owner, :, s + e, pl.ds(a, 16), :].reshape(192, 128) for e in range(2)],
                    axis=1,
                )
                rhs = jnp.concatenate(
                    [xr[:, s + e, pl.ds(a, 16), :].reshape(192, 128) for e in range(2)], axis=1
                )
                acc += lax.dot_general(
                    lhs, rhs, (((1,), (1,)), ((), ())), preferred_element_type=F32
                )
        kept = jnp.where(same, acc, 0.0)
        summed = jnp.sum(kept.reshape(12, 16, 192), axis=1)
        block = jnp.dot(
            summed, pick, preferred_element_type=F32, precision=lax.Precision.HIGHEST
        )
        part[2 * owner, pl.ds(0, 6), :] = block[:6]
        part[2 * owner + 1, pl.ds(0, 6), :] = block[6:]
        return carry

    part[...] = jnp.zeros_like(part)
    lax.fori_loop(0, 8, contract, 0)

    for d in range(1, 16):
        to = (k + d) % 16
        send(part.at[to], red.at[d], rs.at[d], rr.at[d], (g, to))
    total = part[k]
    for d in range(1, 16):
        arrived(red.at[d], rs.at[d], rr.at[d])
        total += red[d]
    out_ref[...] = total[:6, :12] * factor
    for copy in started:
        copy.wait_send()


def per_device(three_centre, occ_green, virt_green, tile_cols, tile_live):
    factor = 1.0 / (128 * math.sqrt(64))
    any_space = pl.BlockSpec(memory_space=pl.ANY)
    smem = pl.BlockSpec(memory_space=pltpu.SMEM)
    dma = pltpu.SemaphoreType.DMA
    return pl.pallas_call(
        functools.partial(kernel, factor),
        out_shape=jax.ShapeDtypeStruct((6, 12), F32),
        in_specs=[smem, smem, any_space, any_space, any_space],
        out_specs=pl.BlockSpec(memory_space=pltpu.VMEM),
        scratch_shapes=[
            pltpu.VMEM((64, 128, 128), BF16),
            pltpu.VMEM((64, 128, 128), BF16),
            pltpu.VMEM((64, 128, 128), BF16),
            pltpu.VMEM((512, 2048), BF16),
            pltpu.VMEM((16, 2048, 128), BF16),
            pltpu.VMEM((8, 12, 4, 128, 128), BF16),
            pltpu.VMEM((512, 2048), BF16),
            pltpu.VMEM((2048, 256), BF16),
            pltpu.VMEM((3, 4, 4, 128, 128), BF16),
            pltpu.VMEM((12, 4, 128, 128), BF16),
            pltpu.VMEM((16, 8, 128), F32),
            pltpu.VMEM((16, 8, 128), F32),
            dma((21,)),
            dma((3, 3)), dma((3, 3)),
            dma((3,)), dma((3,)), dma((3,)), dma((3,)),
            dma((3, 4)), dma((3, 4)), dma((3, 4)), dma((3, 4)),
            dma((3, 4)), dma((3, 4)), dma((3, 4)), dma((3, 4)),
            dma((4,)), dma((4,)), dma((4,)), dma((4,)),
            dma((4,)), dma((4,)),
            dma((4, 4)), dma((4, 4)),
            dma((3, 3)), dma((3, 3)),
            dma((16,)), dma((16,)),
        ],
        compiler_params=pltpu.CompilerParams(
            collective_id=0, has_side_effects=True, vmem_limit_bytes=60 * 1024 * 1024
        ),
    )(tile_cols, tile_live, three_centre, occ_green, virt_green)


def solution(mesh):
    placed = (P("aux", "pair", None, None), P("pair", None), P(), P(), P())
    return jax.shard_map(
        per_device, mesh=mesh, in_specs=placed, out_specs=P("pair", "aux"), check_vma=False
    )
```

```python
import math

import jax
import jax.numpy as jnp
from jax import lax
from jax.experimental import pallas as pl
from jax.experimental.pallas import tpu as pltpu
from jax.sharding import PartitionSpec as P

MESH = pl.DeviceIdType.MESH
F32 = jnp.float32
BF16 = jnp.bfloat16


def kernel(
    cols_ref, live_ref, t_ref, o_ref, v_ref, out_ref,
    tq00, tq01, tq02, tq03, tq10, tq11, tq12, tq13, tq20, tq21, tq22, tq23,
    orow, operm, vv, tp, nn, nacc, dd, stage, xstage, xs, xr, part, red,
    loc, zs, zr, ss, sr, fs, fr, hs, hr, hfs, hfr, ps, pr,
    ysr, yrr, ysl, yrl, fsr, frr, fsl, frl,
    asr, arr, asl, arl, gs, gr, cs, cr, es, er, us, ur, ws, wr, rs, rr,
):
    tqs = ((tq00, tq01, tq02, tq03), (tq10, tq11, tq12, tq13), (tq20, tq21, tq22, tq23))
    g = lax.axis_index("aux")
    k = lax.axis_index("pair")
    y, z = k // 4, k % 4
    x, core = g // 2, g % 2
    partner = (x * 2 + 1 - core, k)
    x_right, x_left, x_far_ = (
        ((x + 1) % 4) * 2 + core, ((x + 3) % 4) * 2 + core, ((x + 2) % 4) * 2 + core,
    )
    y_rel = (y, (y + 3) % 4, (y + 1) % 4, (y + 2) % 4)
    y_right, y_left = (g, y_rel[2] * 4 + z), (g, y_rel[1] * 4 + z)
    z_up, z_down, z_opp = (z + 1) % 4, (z + 3) % 4, (z + 2) % 4
    z_right, z_left = (g, y * 4 + z_up), (g, y * 4 + z_down)

    barrier = pltpu.get_barrier_semaphore()
    peers = [y_right, y_left, z_right, z_left, (x_right, k), (x_left, k), partner]
    for peer in peers:
        pl.semaphore_signal(barrier, inc=1, device_id=peer, device_id_type=MESH)

    started = []

    def local(src, dst, sem):
        copy = pltpu.make_async_copy(src, dst, sem)
        copy.start()
        return copy

    def send(src, dst, send_sem, recv_sem, device):
        copy = pltpu.make_async_remote_copy(
            src_ref=src, dst_ref=dst, send_sem=send_sem, recv_sem=recv_sem,
            device_id=device, device_id_type=MESH,
        )
        copy.start()
        started.append(copy)

    def arrived(dst, send_sem, recv_sem):
        pltpu.make_async_remote_copy(
            src_ref=dst, dst_ref=dst, send_sem=send_sem, recv_sem=recv_sem,
            device_id=partner, device_id_type=MESH,
        ).wait_recv()

    def tiles(q, rel, zi, first=0, count=4):
        return tqs[q][rel].at[pl.ds(4 * zi + first, count)]

    t_local = [local(t_ref.at[3 * z + q], tiles(q, 0, z), loc.at[q]) for q in range(3)]
    o_local = local(o_ref, orow.at[pl.ds(pl.multiple_of(128 * z, 128), 128)], loc.at[4])
    v_local = [
        local(v_ref.at[:, pl.ds(128 * c, 128)], vv.at[c], loc.at[5 + c]) for c in range(16)
    ]
    p_local = local(t_ref, tp.at[g], loc.at[3])
    pl.semaphore_wait(barrier, len(peers))

    def z_sends(q):
        send(t_ref.at[3 * z_up + q], tiles(q, 0, z), zs.at[q, 0], zr.at[q, 0], z_right)
        send(t_ref.at[3 * z_down + q], tiles(q, 0, z), zs.at[q, 1], zr.at[q, 1], z_left)
        opp = 3 * z_opp + q
        send(
            t_ref.at[opp, pl.ds(0, 2)], stage.at[q, 0], ss.at[q, 0], sr.at[q, 0], z_right
        )
        send(t_ref.at[opp, pl.ds(2, 2)], stage.at[q, 1], ss.at[q, 1], sr.at[q, 1], z_left)

    def z_relay(q):
        arrived(stage.at[q, 0], ss.at[q, 0], sr.at[q, 0])
        send(stage.at[q, 0], tiles(q, 0, z_down, 0, 2), fs.at[q, 0], fr.at[q, 0], z_right)
        arrived(stage.at[q, 1], ss.at[q, 1], sr.at[q, 1])
        send(stage.at[q, 1], tiles(q, 0, z_up, 2, 2), fs.at[q, 1], fr.at[q, 1], z_left)

    z_of = (z, z_down, z_opp, z_up)

    def inject(q, d):
        src = tiles(q, 0, z_of[d])
        if d == 0:
            src = t_ref.at[3 * z + q]
        elif d == 1:
            arrived(src, zs.at[q, 0], zr.at[q, 0])
        elif d == 3:
            arrived(src, zs.at[q, 1], zr.at[q, 1])
        else:
            arrived(tiles(q, 0, z_opp, 0, 2), fs.at[q, 0], fr.at[q, 0])
            arrived(tiles(q, 0, z_opp, 2, 2), fs.at[q, 1], fr.at[q, 1])
        send(src, tiles(q, 1, z_of[d]), ysr.at[q, d], yrr.at[q, d], y_right)
        send(src, tiles(q, 2, z_of[d]), ysl.at[q, d], yrl.at[q, d], y_left)

    def relay(q, d):
        zi = z_of[d]
        arrived(tiles(q, 1, zi), ysr.at[q, d], yrr.at[q, d])
        send(
            tiles(q, 1, zi, 0, 2), tiles(q, 3, zi, 0, 2), fsr.at[q, d], frr.at[q, d], y_right
        )
        arrived(tiles(q, 2, zi), ysl.at[q, d], yrl.at[q, d])
        send(
            tiles(q, 2, zi, 2, 2), tiles(q, 3, zi, 2, 2), fsl.at[q, d], frl.at[q, d], y_left
        )

    def far(q, d):
        zi = z_of[d]
        arrived(tiles(q, 3, zi, 0, 2), fsr.at[q, d], frr.at[q, d])
        arrived(tiles(q, 3, zi, 2, 2), fsl.at[q, d], frl.at[q, d])

    def o_at(zi, which, first=0, count=64):
        return orow.at[pl.ds(pl.multiple_of(128 * zi + 64 * which + first, 32), count)]

    def o_sends():
        src = o_ref.at[pl.ds(pl.multiple_of(64 * core, 64), 64)]
        send(src, o_at(z, core), hs.at[0], hr.at[0], z_right)
        send(src, o_at(z, core), hs.at[1], hr.at[1], z_left)

    def o_relay():
        at = o_at(z_down, core, 0, 32)
        arrived(o_at(z_down, core), hs.at[0], hr.at[0])
        send(at, at, hfs.at[0], hfr.at[0], z_right)
        send(o_at(z_down, core), o_at(z_down, core), ps.at[0], pr.at[0], partner)
        at = o_at(z_up, core, 32, 32)
        arrived(o_at(z_up, core), hs.at[1], hr.at[1])
        send(at, at, hfs.at[1], hfr.at[1], z_left)
        send(o_at(z_up, core), o_at(z_up, core), ps.at[1], pr.at[1], partner)

    def o_share():
        arrived(o_at(z_opp, core, 0, 32), hfs.at[0], hfr.at[0])
        arrived(o_at(z_opp, core, 32, 32), hfs.at[1], hfr.at[1])
        send(o_at(z_opp, core), o_at(z_opp, core), ps.at[2], pr.at[2], partner)

    def o_done():
        o_local.wait()
        for n, zi in enumerate((z_down, z_up, z_opp)):
            arrived(o_at(zi, 1 - core), ps.at[n], pr.at[n])
        for rel in range(4):
            at = pl.multiple_of(512 * y_rel[rel], 512)
            operm[:, pl.ds(512 * rel, 512)] = orow[:, pl.ds(at, 512)]

    def chunk(owner, j):
        return tp.at[owner, pl.ds(3 * j, 3)]

    def x_sends(j):
        src = t_ref.at[pl.ds(3 * j, 3)]
        send(src, chunk(g, j), asr.at[j], arr.at[j], (x_right, k))
        send(src, chunk(g, j), asl.at[j], arl.at[j], (x_left, k))
        send(src, chunk(g, j), cs.at[0, j], cr.at[0, j], partner)

    def x_relay(j):
        at = chunk(x_left, j)
        arrived(at, asr.at[j], arr.at[j])
        if j < 2:
            send(at, at, gs.at[j], gr.at[j], (x_right, k))
        send(at, at, cs.at[1, j], cr.at[1, j], partner)
        at = chunk(x_right, j)
        arrived(at, asl.at[j], arl.at[j])
        if j >= 2:
            send(at, at, gs.at[j], gr.at[j], (x_left, k))
        send(at, at, cs.at[2, j], cr.at[2, j], partner)

    def x_far(j):
        at = chunk(x_far_, j)
        arrived(at, gs.at[j], gr.at[j])
        send(at, at, cs.at[3, j], cr.at[3, j], partner)

    def x_done(j):
        for n, dx in enumerate((0, 3, 1, 2)):
            owner = ((x + dx) % 4) * 2 + 1 - core
            arrived(chunk(owner, j), cs.at[n, j], cr.at[n, j])

    def fill(q, rels, pair):
        for h in range(2):
            c = 2 * pair + h
            for rel in rels:
                tq = tqs[q][rel]
                for zi in range(4):
                    i = 4 * y_rel[rel] + zi
                    c0, c1, c2, c3 = (cols_ref[s, i] for s in range(4))
                    s = jnp.where(c1 == c, 1, jnp.where(c2 == c, 2, jnp.where(c3 == c, 3, 0)))
                    hit = (c0 == c) | (c1 == c) | (c2 == c) | (c3 == c)
                    keep = hit & (s < live_ref[i])
                    tile = tq[4 * zi + s]
                    dd[pl.ds(512 * rel + 128 * zi, 128), pl.ds(128 * h, 128)] = jnp.where(
                        keep, tile, jnp.zeros_like(tile)
                    )

    def product(rels):
        span = pl.ds(512 * rels[0], 512 * len(rels))
        return jnp.dot(operm[:, span], dd[span, :], preferred_element_type=F32)

    def n_part(q, lo, hi, rels=(0, 1, 2, 3)):
        def columns(pair, carry):
            fill(q, rels, pair)
            acc = product(rels)
            at = pl.ds(pl.multiple_of(256 * pair, 256), 256)
            if rels[0]:
                acc += nacc[:, at]
            if rels[-1] == 3:
                nn[:, at] = acc.astype(BF16)
            else:
                nacc[:, at] = acc
            return carry

        lax.fori_loop(lo, hi, columns, 0)

    def x_rows(q, r, dst):
        lhs = nn[pl.ds(pl.multiple_of(128 * r, 128), 128), :]
        i = 4 * y + r
        for s in range(0, 4, 2):
            rhs = jnp.concatenate([vv[cols_ref[s + e, i]] for e in range(2)], axis=1)
            acc = jnp.dot(lhs, rhs, preferred_element_type=F32)
            for e in range(2):
                tile = acc[:, 128 * e : 128 * e + 128]
                dst[s + e] = jnp.where(s + e < live_ref[i], tile, 0.0).astype(BF16)

    def e_opp(q):
        src = xs.at[q, z_opp]
        send(src.at[pl.ds(0, 2)], xstage.at[q, 0], us.at[q, 0], ur.at[q, 0], z_right)
        send(src.at[pl.ds(2, 2)], xstage.at[q, 1], us.at[q, 1], ur.at[q, 1], z_left)

    def e_up(q):
        send(xs.at[q, z_up], xr.at[3 * z + q], es.at[q, 0], er.at[q, 0], z_right)

    def e_down(q):
        send(xs.at[q, z_down], xr.at[3 * z + q], es.at[q, 1], er.at[q, 1], z_left)

    def e_relay(q):
        at = xstage.at[q, 0]
        arrived(at, us.at[q, 0], ur.at[q, 0])
        send(at, xr.at[3 * z_down + q, pl.ds(0, 2)], ws.at[q, 0], wr.at[q, 0], z_right)
        at = xstage.at[q, 1]
        arrived(at, us.at[q, 1], ur.at[q, 1])
        send(at, xr.at[3 * z_up + q, pl.ds(2, 2)], ws.at[q, 1], wr.at[q, 1], z_left)

    def e_done(q):
        arrived(xr.at[3 * z_down + q], es.at[q, 0], er.at[q, 0])
        arrived(xr.at[3 * z_up + q], es.at[q, 1], er.at[q, 1])
        arrived(xr.at[3 * z_opp + q, pl.ds(0, 2)], ws.at[q, 0], wr.at[q, 0])
        arrived(xr.at[3 * z_opp + q, pl.ds(2, 2)], ws.at[q, 1], wr.at[q, 1])

    def x_part(q):
        x_rows(q, z_opp, xs.at[q, z_opp])
        x_rows(q, z_up, xs.at[q, z_up])
        e_opp(q)
        x_rows(q, z_down, xs.at[q, z_down])
        e_up(q)
        x_rows(q, z, xr.at[3 * z + q])
        e_down(q)

    z_sends(0)
    inject(0, 0)
    x_sends(0)
    inject(1, 0)
    z_sends(1)
    o_sends()
    z_sends(2)
    x_sends(1)
    x_sends(2)
    x_sends(3)
    z_relay(0)
    inject(0, 1)
    inject(0, 3)
    relay(0, 0)
    inject(0, 2)
    z_relay(1)
    relay(0, 1)
    relay(0, 3)
    x_relay(0)
    relay(0, 2)
    o_relay()
    inject(1, 1)
    inject(1, 3)
    relay(1, 0)
    inject(1, 2)
    z_relay(2)
    o_share()
    x_relay(1)
    inject(2, 0)
    for d in range(4):
        far(0, d)
    o_done()
    for copy in t_local + v_local:
        copy.wait()
    n_part(0, 0, 2)
    relay(1, 1)
    inject(2, 1)
    n_part(0, 2, 4)
    relay(1, 3)
    inject(2, 3)
    n_part(0, 4, 6)
    relay(1, 2)
    inject(2, 2)
    x_relay(2)
    n_part(0, 6, 8)
    relay(2, 0)
    x_far(0)
    x_part(0)
    x_relay(3)
    for d in range(4):
        far(1, d)
    e_relay(0)
    n_part(1, 0, 4)
    relay(2, 1)
    x_far(1)
    n_part(1, 4, 8)
    relay(2, 3)
    x_part(1)
    relay(2, 2)
    n_part(2, 0, 8, (0, 1, 2))
    e_relay(1)
    x_far(2)
    for d in range(4):
        far(2, d)
    n_part(2, 0, 8, (3,))
    x_part(2)
    x_far(3)
    e_relay(2)
    for j in range(4):
        x_done(j)
    p_local.wait()
    for q in range(3):
        e_done(q)

    row = lax.broadcasted_iota(jnp.int32, (192, 192), 0)
    col = lax.broadcasted_iota(jnp.int32, (192, 192), 1)
    same = (row % 16) == (col % 16)
    pick = (
        lax.broadcasted_iota(jnp.int32, (192, 128), 0) // 16
        == lax.broadcasted_iota(jnp.int32, (192, 128), 1)
    ).astype(F32)

    def contract(owner, carry):
        acc = jnp.zeros((192, 192), F32)
        for s in range(0, 4, 2):
            for a in range(0, 128, 16):
                lhs = jnp.concatenate(
                    [tp[owner, :, s + e, pl.ds(a, 16), :].reshape(192, 128) for e in range(2)],
                    axis=1,
                )
                rhs = jnp.concatenate(
                    [xr[:, s + e, pl.ds(a, 16), :].reshape(192, 128) for e in range(2)], axis=1
                )
                acc += lax.dot_general(
                    lhs, rhs, (((1,), (1,)), ((), ())), preferred_element_type=F32
                )
        kept = jnp.where(same, acc, 0.0)
        summed = jnp.sum(kept.reshape(12, 16, 192), axis=1)
        block = jnp.dot(
            summed, pick, preferred_element_type=F32, precision=lax.Precision.HIGHEST
        )
        part[2 * owner, pl.ds(0, 6), :] = block[:6]
        part[2 * owner + 1, pl.ds(0, 6), :] = block[6:]
        return carry

    part[...] = jnp.zeros_like(part)
    lax.fori_loop(0, 8, contract, 0)

    for d in range(1, 16):
        to = (k + d) % 16
        send(part.at[to], red.at[d], rs.at[d], rr.at[d], (g, to))
    total = part[k]
    for d in range(1, 16):
        arrived(red.at[d], rs.at[d], rr.at[d])
        total += red[d]
    out_ref[...] = total[:6, :12]
    for copy in started:
        copy.wait_send()


def per_device(three_centre, occ_green, virt_green, tile_cols, tile_live):
    factor = 1.0 / (128 * math.sqrt(64))
    any_space = pl.BlockSpec(memory_space=pl.ANY)
    smem = pl.BlockSpec(memory_space=pltpu.SMEM)
    dma = pltpu.SemaphoreType.DMA
    chi = pl.pallas_call(
        kernel,
        out_shape=jax.ShapeDtypeStruct((6, 12), F32),
        in_specs=[smem, smem, any_space, any_space, any_space],
        out_specs=pl.BlockSpec(memory_space=pltpu.VMEM),
        scratch_shapes=[pltpu.VMEM((16, 128, 128), BF16)] * 12
        + [
            pltpu.VMEM((512, 2048), BF16),
            pltpu.VMEM((512, 2048), BF16),
            pltpu.VMEM((16, 2048, 128), BF16),
            pltpu.VMEM((8, 12, 4, 128, 128), BF16),
            pltpu.VMEM((512, 2048), BF16),
            pltpu.VMEM((512, 2048), F32),
            pltpu.VMEM((2048, 256), BF16),
            pltpu.VMEM((3, 2, 2, 128, 128), BF16),
            pltpu.VMEM((3, 2, 2, 128, 128), BF16),
            pltpu.VMEM((3, 4, 4, 128, 128), BF16),
            pltpu.VMEM((12, 4, 128, 128), BF16),
            pltpu.VMEM((16, 8, 128), F32),
            pltpu.VMEM((16, 8, 128), F32),
            dma((21,)),
            dma((3, 2)), dma((3, 2)), dma((3, 2)), dma((3, 2)), dma((3, 2)), dma((3, 2)),
            dma((2,)), dma((2,)), dma((2,)), dma((2,)), dma((3,)), dma((3,)),
            dma((3, 4)), dma((3, 4)), dma((3, 4)), dma((3, 4)),
            dma((3, 4)), dma((3, 4)), dma((3, 4)), dma((3, 4)),
            dma((4,)), dma((4,)), dma((4,)), dma((4,)), dma((4,)), dma((4,)),
            dma((4, 4)), dma((4, 4)),
            dma((3, 2)), dma((3, 2)), dma((3, 2)), dma((3, 2)), dma((3, 2)), dma((3, 2)),
            dma((16,)), dma((16,)),
        ],
        compiler_params=pltpu.CompilerParams(
            collective_id=0, has_side_effects=True, vmem_limit_bytes=60 * 1024 * 1024
        ),
    )(tile_cols.T, tile_live, three_centre, occ_green, virt_green)
    return chi * factor


def solution(mesh):
    placed = (P("aux", "pair", None, None), P("pair", None), P(), P(), P())
    return jax.shard_map(
        per_device, mesh=mesh, in_specs=placed, out_specs=P("pair", "aux"), check_vma=False
    )
```

```python
import math

import jax
import jax.numpy as jnp
from jax import lax
from jax.experimental import pallas as pl
from jax.experimental.pallas import tpu as pltpu
from jax.sharding import PartitionSpec as P

MESH = pl.DeviceIdType.MESH
F32 = jnp.float32
BF16 = jnp.bfloat16


def kernel(
    cols_ref, live_ref, t_ref, o_ref, v_ref, out_ref,
    tq00, tq01, tq02, tq03, tq10, tq11, tq12, tq13, tq20, tq21, tq22, tq23,
    orow, operm, vv, tp, nn, nacc, big0, big1, stage, xstage, xs, xr, cacc, dsum, part, red, table,
    loc, zs, zr, ss, sr, fs, fr, hs, hr, hfs, hfr,
    ysr, yrr, ysl, yrl, fsr, frr, fsl, frl,
    asr, arr, asl, arl, gs, gr, cs, cr, es, er, us, ur, ws, wr, rs, rr,
):
    tqs = ((tq00, tq01, tq02, tq03), (tq10, tq11, tq12, tq13), (tq20, tq21, tq22, tq23))
    g = lax.axis_index("aux")
    k = lax.axis_index("pair")
    y, z = k // 4, k % 4
    x, core = g // 2, g % 2
    partner = (x * 2 + 1 - core, k)
    x_right, x_left, x_far_ = (
        ((x + 1) % 4) * 2 + core, ((x + 3) % 4) * 2 + core, ((x + 2) % 4) * 2 + core,
    )
    ring, sub = y + core * (z - y), z + core * (y - z)
    ring_step, sub_step = 4 - 3 * core, 1 + 3 * core

    def block(r, u):
        return r * ring_step + u * sub_step

    r_rel = (ring, (ring + 3) % 4, (ring + 1) % 4, (ring + 2) % 4)
    r_right, r_left = (g, block(r_rel[2], sub)), (g, block(r_rel[1], sub))
    u_up, u_down, u_opp = (sub + 1) % 4, (sub + 3) % 4, (sub + 2) % 4
    u_right, u_left = (g, block(ring, u_up)), (g, block(ring, u_down))
    u_across = (g, block(ring, u_opp))

    barrier = pltpu.get_barrier_semaphore()
    peers = [r_right, r_left, u_right, u_left, (x_right, k), (x_left, k), partner]
    for peer in peers:
        pl.semaphore_signal(barrier, inc=1, device_id=peer, device_id_type=MESH)

    started = []

    def local(src, dst, sem):
        copy = pltpu.make_async_copy(src, dst, sem)
        copy.start()
        return copy

    def send(src, dst, send_sem, recv_sem, device):
        copy = pltpu.make_async_remote_copy(
            src_ref=src, dst_ref=dst, send_sem=send_sem, recv_sem=recv_sem,
            device_id=device, device_id_type=MESH,
        )
        copy.start()
        started.append(copy)

    def arrived(dst, send_sem, recv_sem):
        pltpu.make_async_remote_copy(
            src_ref=dst, dst_ref=dst, send_sem=send_sem, recv_sem=recv_sem,
            device_id=partner, device_id_type=MESH,
        ).wait_recv()

    def tiles(q, rel, zi, first=0, count=4):
        return tqs[q][rel].at[pl.ds(4 * zi + first, count)]

    t_local = [local(t_ref.at[3 * sub + q], tiles(q, 0, sub), loc.at[q]) for q in range(3)]
    o_local = local(o_ref, orow.at[pl.ds(pl.multiple_of(128 * sub, 128), 128)], loc.at[4])
    v_local = [
        local(v_ref.at[:, pl.ds(128 * c, 128)], vv.at[c], loc.at[5 + c]) for c in range(16)
    ]
    p_local = local(t_ref, tp.at[g], loc.at[3])
    pl.semaphore_wait(barrier, len(peers))

    def z_sends(q):
        opp = 3 * u_opp + q
        send(
            t_ref.at[opp, pl.ds(0, 2)], stage.at[q, 0], ss.at[q, 0], sr.at[q, 0], u_right
        )
        send(t_ref.at[opp, pl.ds(2, 2)], stage.at[q, 1], ss.at[q, 1], sr.at[q, 1], u_left)
        send(t_ref.at[3 * u_up + q], tiles(q, 0, sub), zs.at[q, 0], zr.at[q, 0], u_right)
        send(t_ref.at[3 * u_down + q], tiles(q, 0, sub), zs.at[q, 1], zr.at[q, 1], u_left)

    def z_relay(q):
        arrived(stage.at[q, 0], ss.at[q, 0], sr.at[q, 0])
        send(stage.at[q, 0], tiles(q, 0, u_down, 0, 2), fs.at[q, 0], fr.at[q, 0], u_right)
        arrived(stage.at[q, 1], ss.at[q, 1], sr.at[q, 1])
        send(stage.at[q, 1], tiles(q, 0, u_up, 2, 2), fs.at[q, 1], fr.at[q, 1], u_left)

    z_of = (sub, u_down, u_opp, u_up)

    def inject(q, d):
        src = tiles(q, 0, z_of[d])
        if d == 0:
            src = t_ref.at[3 * sub + q]
        elif d == 1:
            arrived(src, zs.at[q, 0], zr.at[q, 0])
        elif d == 3:
            arrived(src, zs.at[q, 1], zr.at[q, 1])
        else:
            arrived(tiles(q, 0, u_opp, 0, 2), fs.at[q, 0], fr.at[q, 0])
            arrived(tiles(q, 0, u_opp, 2, 2), fs.at[q, 1], fr.at[q, 1])
        send(src, tiles(q, 1, z_of[d]), ysr.at[q, d], yrr.at[q, d], r_right)
        send(src, tiles(q, 2, z_of[d]), ysl.at[q, d], yrl.at[q, d], r_left)

    def relay(q, d):
        zi = z_of[d]
        arrived(tiles(q, 1, zi), ysr.at[q, d], yrr.at[q, d])
        send(
            tiles(q, 1, zi, 0, 2), tiles(q, 3, zi, 0, 2), fsr.at[q, d], frr.at[q, d], r_right
        )
        arrived(tiles(q, 2, zi), ysl.at[q, d], yrl.at[q, d])
        send(
            tiles(q, 2, zi, 2, 2), tiles(q, 3, zi, 2, 2), fsl.at[q, d], frl.at[q, d], r_left
        )

    def far(q, d):
        zi = z_of[d]
        arrived(tiles(q, 3, zi, 0, 2), fsr.at[q, d], frr.at[q, d])
        arrived(tiles(q, 3, zi, 2, 2), fsl.at[q, d], frl.at[q, d])

    def o_at(zi, first=0, count=128):
        return orow.at[pl.ds(pl.multiple_of(128 * zi + first, 64), count)]

    def o_sends(h):
        right, left = 64 * h, 64 - 64 * h
        send(
            o_ref.at[pl.ds(right, 64)], o_at(sub, right, 64), hs.at[0, h], hr.at[0, h], u_right
        )
        send(o_ref.at[pl.ds(left, 64)], o_at(sub, left, 64), hs.at[1, h], hr.at[1, h], u_left)

    def o_relay():
        at = o_at(u_down, 0, 64)
        arrived(at, hs.at[0, 0], hr.at[0, 0])
        send(at, at, hfs.at[0], hfr.at[0], u_right)
        at = o_at(u_up, 64, 64)
        arrived(at, hs.at[1, 0], hr.at[1, 0])
        send(at, at, hfs.at[1], hfr.at[1], u_left)

    def o_perm(r):
        rows = pl.ds(pl.multiple_of(128 * r, 128), 128)
        for rel in range(4):
            for u in range(4):
                at = pl.multiple_of(128 * block(r_rel[rel], u), 128)
                operm[rows, pl.ds(512 * rel + 128 * u, 128)] = orow[rows, pl.ds(at, 128)]

    def o_near():
        arrived(o_at(u_down, 64, 64), hs.at[0, 1], hr.at[0, 1])
        arrived(o_at(u_up, 0, 64), hs.at[1, 1], hr.at[1, 1])
        o_perm(u_down)
        o_perm(u_up)

    def o_far():
        arrived(o_at(u_opp, 0, 64), hfs.at[0], hfr.at[0])
        arrived(o_at(u_opp, 64, 64), hfs.at[1], hfr.at[1])
        o_perm(u_opp)

    def chunk(owner, j):
        return tp.at[owner, pl.ds(3 * j, 3)]

    def x_sends(t):
        j, opp = t, (t + 2) % 4
        send(t_ref.at[pl.ds(3 * j, 3)], chunk(g, j), asr.at[j], arr.at[j], (x_right, k))
        send(t_ref.at[pl.ds(3 * opp, 3)], chunk(g, opp), asl.at[opp], arl.at[opp], (x_left, k))
        send(t_ref.at[pl.ds(3 * j, 3)], chunk(g, j), cs.at[0, j], cr.at[0, j], partner)

    def x_relay(t):
        j, opp = t, (t + 2) % 4
        at = chunk(x_left, j)
        arrived(at, asr.at[j], arr.at[j])
        if t < 2:
            send(at, at, gs.at[j], gr.at[j], (x_right, k))
        send(at, at, cs.at[1, j], cr.at[1, j], partner)
        at = chunk(x_right, opp)
        arrived(at, asl.at[opp], arl.at[opp])
        if t < 2:
            send(at, at, gs.at[opp], gr.at[opp], (x_left, k))
        send(at, at, cs.at[2, opp], cr.at[2, opp], partner)

    def x_far(t):
        for j in (t, t + 2):
            at = chunk(x_far_, j)
            arrived(at, gs.at[j], gr.at[j])
            send(at, at, cs.at[3, j], cr.at[3, j], partner)

    def x_done(j):
        for n, dx in enumerate((0, 3, 1, 2)):
            owner = ((x + dx) % 4) * 2 + 1 - core
            arrived(chunk(owner, j), cs.at[n, j], cr.at[n, j])

    def tabulate():
        for q in range(3):
            for rel in range(4):
                tqs[q][rel][16] = jnp.zeros((128, 128), BF16)
        for rel in range(4):

            def unit(u, carry):
                i = block(r_rel[rel], u)
                c0, c1, c2, c3 = (cols_ref[s, i] for s in range(4))
                n_live = live_ref[i]
                for c in range(16):
                    s = jnp.where(c1 == c, 1, jnp.where(c2 == c, 2, jnp.where(c3 == c, 3, 0)))
                    hit = (c0 == c) | (c1 == c) | (c2 == c) | (c3 == c)
                    table[64 * rel + 16 * u + c] = jnp.where(hit & (s < n_live), 4 * u + s, 16)
                return carry

            lax.fori_loop(0, 4, unit, 0)

    def fill_rel(q, rel):
        dst = (big0, big1, big0)[q]

        def unit(u, carry):
            at = pl.multiple_of(512 * rel + 128 * u, 128)
            for c in range(16):
                tile = tqs[q][rel][table[64 * rel + 16 * u + c]]
                dst[pl.ds(at, 128), pl.ds(128 * c, 128)] = tile
            return carry

        lax.fori_loop(0, 4, unit, 0)

    def rows_product(blocks):
        for c in range(0, 2048, 256):
            for r in blocks:
                rows = pl.ds(pl.multiple_of(128 * r, 128), 128)
                acc = jnp.dot(
                    operm[rows, :], big0[:, pl.ds(c, 256)], preferred_element_type=F32
                )
                nn[rows, pl.ds(c, 256)] = acc.astype(BF16)

    def product(lo, hi):
        for c in range(256 * lo, 256 * hi, 256):
            acc = jnp.dot(
                operm[:, pl.ds(0, 1536)], big1[pl.ds(0, 1536), pl.ds(c, 256)],
                preferred_element_type=F32,
            )
            acc += jnp.dot(
                operm[:, pl.ds(1536, 512)], big1[pl.ds(1536, 512), pl.ds(c, 256)],
                preferred_element_type=F32,
            )
            nn[:, pl.ds(c, 256)] = acc.astype(BF16)

    def early_product():
        for c in range(0, 2048, 256):
            nacc[:, pl.ds(c, 256)] = jnp.dot(
                operm[:, pl.ds(0, 1536)], big0[pl.ds(0, 1536), pl.ds(c, 256)],
                preferred_element_type=F32,
            )

    def late_product():
        for c in range(0, 2048, 256):
            acc = nacc[:, pl.ds(c, 256)] + jnp.dot(
                operm[:, pl.ds(1536, 512)], big0[pl.ds(1536, 512), pl.ds(c, 256)],
                preferred_element_type=F32,
            )
            nn[:, pl.ds(c, 256)] = acc.astype(BF16)

    def x_rows(r, dst, first):
        lhs = nn[pl.ds(pl.multiple_of(128 * r, 128), 128), :]
        i = block(ring, r)
        rhs = jnp.concatenate([vv[cols_ref[first + e, i]] for e in range(2)], axis=1)
        acc = jnp.dot(lhs, rhs, preferred_element_type=F32)
        for e in range(2):
            tile = acc[:, 128 * e : 128 * e + 128]
            dst[first + e] = jnp.where(first + e < live_ref[i], tile, 0.0).astype(BF16)

    def piece(m):
        q = min(m, 2)
        first, count = (0, 4) if m < 2 else (2 * m - 4, 2)
        return q, first, first + count // 2, count // 2

    def e_opp(m):
        q, a, b, n = piece(m)
        src = xs.at[q, u_opp]
        if m >= 2:
            at = pl.ds(a, 2 * n)
            send(src.at[at], xr.at[q, sub, at], us.at[m, 0], ur.at[m, 0], u_across)
            return
        lo, hi = xstage.at[m, 0, pl.ds(0, n)], xstage.at[m, 1, pl.ds(0, n)]
        send(src.at[pl.ds(a, n)], lo, us.at[m, 0], ur.at[m, 0], u_right)
        send(src.at[pl.ds(b, n)], hi, us.at[m, 1], ur.at[m, 1], u_left)

    def e_up(m):
        q, a, b, n = piece(m)
        at = pl.ds(a, 2 * n)
        send(xs.at[q, u_up, at], xr.at[q, sub, at], es.at[m, 0], er.at[m, 0], u_right)

    def e_down(m):
        q, a, b, n = piece(m)
        at = pl.ds(a, 2 * n)
        send(xs.at[q, u_down, at], xr.at[q, sub, at], es.at[m, 1], er.at[m, 1], u_left)

    def e_relay(m):
        q, a, b, n = piece(m)
        at = xstage.at[m, 0, pl.ds(0, n)]
        arrived(at, us.at[m, 0], ur.at[m, 0])
        send(at, xr.at[q, u_down, pl.ds(a, n)], ws.at[m, 0], wr.at[m, 0], u_right)
        at = xstage.at[m, 1, pl.ds(0, n)]
        arrived(at, us.at[m, 1], ur.at[m, 1])
        send(at, xr.at[q, u_up, pl.ds(b, n)], ws.at[m, 1], wr.at[m, 1], u_left)

    def e_done(m):
        q, a, b, n = piece(m)
        at = pl.ds(a, 2 * n)
        arrived(xr.at[q, u_down, at], es.at[m, 0], er.at[m, 0])
        arrived(xr.at[q, u_up, at], es.at[m, 1], er.at[m, 1])
        if m >= 2:
            arrived(xr.at[q, u_opp, at], us.at[m, 0], ur.at[m, 0])
            return
        arrived(xr.at[q, u_opp, pl.ds(a, n)], ws.at[m, 0], wr.at[m, 0])
        arrived(xr.at[q, u_opp, pl.ds(b, n)], ws.at[m, 1], wr.at[m, 1])

    def x_part(m):
        q, a, b, n = piece(m)
        for r in (u_opp, u_up, u_down, sub):
            dst = xr.at[q, sub] if r is sub else xs.at[q, r]
            for first in (0, 2) if n == 2 else (a,):
                x_rows(r, dst, first)
        e_opp(m)
        e_up(m)
        e_down(m)

    def contract(h):
        def body(n, carry):
            lhs, rhs = [], []
            for e in range(2):
                a = pl.multiple_of(32 * n + 16 * e, 16)
                for s in (2 * h, 2 * h + 1):
                    lhs.append(tp[:, :, s, pl.ds(a, 16), :].reshape(1536, 128))
                    rhs.append(xr[:, :, s, pl.ds(a, 16), :].reshape(192, 128))
            cacc[...] += lax.dot_general(
                jnp.concatenate(lhs, axis=1), jnp.concatenate(rhs, axis=1),
                (((1,), (1,)), ((), ())), preferred_element_type=F32,
            )
            return carry

        lax.fori_loop(0, 4, body, 0)

    z_sends(0)
    inject(0, 0)
    x_sends(0)
    inject(1, 0)
    inject(2, 0)
    z_relay(0)
    inject(0, 1)
    inject(0, 3)
    z_sends(1)
    inject(0, 2)
    relay(0, 0)
    x_sends(1)
    x_sends(2)
    x_sends(3)
    for copy in t_local + v_local:
        copy.wait()
    o_local.wait()
    o_perm(sub)
    o_sends(0)
    z_relay(1)
    tabulate()
    relay(0, 1)
    relay(0, 3)
    fill_rel(0, 0)
    relay(0, 2)
    o_sends(1)
    relay(1, 0)
    x_relay(0)
    inject(1, 1)
    inject(1, 3)
    fill_rel(0, 1)
    inject(1, 2)
    o_relay()
    z_sends(2)
    relay(2, 0)
    fill_rel(0, 2)
    x_relay(1)
    for d in range(4):
        far(0, d)
    fill_rel(0, 3)
    rows_product([sub])
    fill_rel(1, 0)
    relay(1, 1)
    relay(1, 3)
    o_near()
    rows_product([u_down, u_up])
    x_relay(2)
    relay(1, 2)
    fill_rel(1, 1)
    fill_rel(1, 2)
    o_far()
    z_relay(2)
    rows_product([u_opp])
    inject(2, 1)
    inject(2, 3)
    x_part(0)
    for d in range(4):
        far(1, d)
    fill_rel(1, 3)
    product(0, 2)
    inject(2, 2)
    product(2, 4)
    product(4, 6)
    relay(2, 1)
    product(6, 8)
    fill_rel(2, 0)
    relay(2, 3)
    x_relay(3)
    relay(2, 2)
    e_relay(0)
    x_part(1)
    fill_rel(2, 1)
    fill_rel(2, 2)
    early_product()
    x_far(0)
    e_relay(1)
    for d in range(4):
        far(2, d)
    fill_rel(2, 3)
    late_product()
    x_part(2)
    x_part(3)
    x_far(1)
    cacc[...] = jnp.zeros_like(cacc)
    dsum[...] = jnp.zeros_like(dsum)
    part[...] = jnp.zeros_like(part)
    e_done(0)
    e_done(1)
    e_done(2)
    for j in range(4):
        x_done(j)
    p_local.wait()
    contract(0)
    e_done(3)
    contract(1)
    row = lax.broadcasted_iota(jnp.int32, (192, 192), 0)
    col = lax.broadcasted_iota(jnp.int32, (192, 192), 1)
    same = (row % 16) == (col % 16)
    row = lax.broadcasted_iota(jnp.int32, (192, 128), 0)
    col = lax.broadcasted_iota(jnp.int32, (192, 128), 1)
    pick = (3 * (row // 16 % 4) + row // 64 == col).astype(F32)
    for owner in range(8):
        kept = jnp.where(same, cacc[pl.ds(192 * owner, 192), :], 0.0)
        dsum[owner, pl.ds(0, 12), :] = jnp.sum(kept.reshape(12, 16, 192), axis=1)
    summed = jnp.dot(
        dsum[...].reshape(128, 192), pick,
        preferred_element_type=F32, precision=lax.Precision.HIGHEST,
    ).reshape(8, 16, 128)
    for owner in range(8):
        part[2 * owner, pl.ds(0, 6), :] = summed[owner, :6]
        part[2 * owner + 1, pl.ds(0, 6), :] = summed[owner, 6:12]

    for d in range(1, 16):
        to = (k + d) % 16
        send(part.at[to], red.at[d], rs.at[d], rr.at[d], (g, to))
    total = part[k]
    for d in range(1, 16):
        arrived(red.at[d], rs.at[d], rr.at[d])
        total += red[d]
    out_ref[...] = total[:6, :12]
    for copy in started:
        copy.wait_send()


def per_device(three_centre, occ_green, virt_green, tile_cols, tile_live):
    factor = 1.0 / (128 * math.sqrt(64))
    any_space = pl.BlockSpec(memory_space=pl.ANY)
    smem = pl.BlockSpec(memory_space=pltpu.SMEM)
    dma = pltpu.SemaphoreType.DMA
    chi = pl.pallas_call(
        kernel,
        out_shape=jax.ShapeDtypeStruct((6, 12), F32),
        in_specs=[smem, smem, any_space, any_space, any_space],
        out_specs=pl.BlockSpec(memory_space=pltpu.VMEM),
        scratch_shapes=[pltpu.VMEM((17, 128, 128), BF16)] * 12
        + [
            pltpu.VMEM((512, 2048), BF16),
            pltpu.VMEM((512, 2048), BF16),
            pltpu.VMEM((16, 2048, 128), BF16),
            pltpu.VMEM((8, 12, 4, 128, 128), BF16),
            pltpu.VMEM((512, 2048), BF16),
            pltpu.VMEM((512, 2048), F32),
            pltpu.VMEM((2048, 2048), BF16),
            pltpu.VMEM((2048, 2048), BF16),
            pltpu.VMEM((3, 2, 2, 128, 128), BF16),
            pltpu.VMEM((4, 2, 2, 128, 128), BF16),
            pltpu.VMEM((3, 4, 4, 128, 128), BF16),
            pltpu.VMEM((3, 4, 4, 128, 128), BF16),
            pltpu.VMEM((1536, 192), F32),
            pltpu.VMEM((8, 16, 192), F32),
            pltpu.VMEM((16, 8, 128), F32),
            pltpu.VMEM((16, 8, 128), F32),
            pltpu.SMEM((256,), jnp.int32),
            dma((21,)),
            dma((3, 2)), dma((3, 2)), dma((3, 2)), dma((3, 2)), dma((3, 2)), dma((3, 2)),
            dma((2, 2)), dma((2, 2)), dma((2,)), dma((2,)),
            dma((3, 4)), dma((3, 4)), dma((3, 4)), dma((3, 4)),
            dma((3, 4)), dma((3, 4)), dma((3, 4)), dma((3, 4)),
            dma((4,)), dma((4,)), dma((4,)), dma((4,)), dma((4,)), dma((4,)),
            dma((4, 4)), dma((4, 4)),
            dma((4, 2)), dma((4, 2)), dma((4, 2)), dma((4, 2)), dma((4, 2)), dma((4, 2)),
            dma((16,)), dma((16,)),
        ],
        compiler_params=pltpu.CompilerParams(
            collective_id=0, has_side_effects=True, vmem_limit_bytes=67043328
        ),
    )(tile_cols.T, tile_live, three_centre, occ_green, virt_green)
    return chi * factor


def solution(mesh):
    placed = (P("aux", "pair", None, None), P("pair", None), P(), P(), P())
    return jax.shard_map(
        per_device, mesh=mesh, in_specs=placed, out_specs=P("pair", "aux"), check_vma=False
    )
```

```python
import math

import jax
import jax.numpy as jnp
from jax import lax
from jax.experimental import pallas as pl
from jax.experimental.pallas import tpu as pltpu
from jax.sharding import PartitionSpec as P

MESH = pl.DeviceIdType.MESH
F32 = jnp.float32
BF16 = jnp.bfloat16


def kernel(
    cols_ref, live_ref, t_ref, o_ref, v_ref, out_ref,
    tq00, tq01, tq02, tq03, tq10, tq11, tq12, tq13, tq20, tq21, tq22, tq23,
    orow, operm, vv, tp, nn, nacc, big0, big1, stage, xstage, xs, xr, cacc, dsum, part, red, table,
    loc, zs, zr, ss, sr, fs, fr, hs, hr, hfs, hfr,
    ysr, yrr, ysl, yrl, fsr, frr, fsl, frl,
    asr, arr, asl, arl, gs, gr, cs, cr, es, er, us, ur, ws, wr, rs, rr,
):
    tqs = ((tq00, tq01, tq02, tq03), (tq10, tq11, tq12, tq13), (tq20, tq21, tq22, tq23))
    g = lax.axis_index("aux")
    k = lax.axis_index("pair")
    y, z = k // 4, k % 4
    x, core = g // 2, g % 2
    partner = (x * 2 + 1 - core, k)
    x_right, x_left, x_far_ = (
        ((x + 1) % 4) * 2 + core, ((x + 3) % 4) * 2 + core, ((x + 2) % 4) * 2 + core,
    )
    ring, sub = y + core * (z - y), z + core * (y - z)
    ring_step, sub_step = 4 - 3 * core, 1 + 3 * core

    def block(r, u):
        return r * ring_step + u * sub_step

    r_rel = (ring, (ring + 3) % 4, (ring + 1) % 4, (ring + 2) % 4)
    r_right, r_left = (g, block(r_rel[2], sub)), (g, block(r_rel[1], sub))
    u_up, u_down, u_opp = (sub + 1) % 4, (sub + 3) % 4, (sub + 2) % 4
    u_right, u_left = (g, block(ring, u_up)), (g, block(ring, u_down))
    u_across = (g, block(ring, u_opp))

    barrier = pltpu.get_barrier_semaphore()
    peers = [r_right, r_left, u_right, u_left, (x_right, k), (x_left, k), partner]
    for peer in peers:
        pl.semaphore_signal(barrier, inc=1, device_id=peer, device_id_type=MESH)

    started = []

    def local(src, dst, sem):
        copy = pltpu.make_async_copy(src, dst, sem)
        copy.start()
        return copy

    def send(src, dst, send_sem, recv_sem, device):
        copy = pltpu.make_async_remote_copy(
            src_ref=src, dst_ref=dst, send_sem=send_sem, recv_sem=recv_sem,
            device_id=device, device_id_type=MESH,
        )
        copy.start()
        started.append(copy)

    def arrived(dst, send_sem, recv_sem):
        pltpu.make_async_remote_copy(
            src_ref=dst, dst_ref=dst, send_sem=send_sem, recv_sem=recv_sem,
            device_id=partner, device_id_type=MESH,
        ).wait_recv()

    def tiles(q, rel, zi, first=0, count=4):
        return tqs[q][rel].at[pl.ds(4 * zi + first, count)]

    t_local = [local(t_ref.at[3 * sub + q], tiles(q, 0, sub), loc.at[q]) for q in range(3)]
    o_local = local(o_ref, orow.at[pl.ds(pl.multiple_of(128 * sub, 128), 128)], loc.at[4])
    v_local = [
        local(v_ref.at[:, pl.ds(128 * c, 128)], vv.at[c], loc.at[5 + c]) for c in range(16)
    ]
    p_local = local(t_ref, tp.at[g], loc.at[3])
    pl.semaphore_wait(barrier, len(peers))

    def z_sends(q):
        opp = 3 * u_opp + q
        send(
            t_ref.at[opp, pl.ds(0, 2)], stage.at[q, 0], ss.at[q, 0], sr.at[q, 0], u_right
        )
        send(t_ref.at[opp, pl.ds(2, 2)], stage.at[q, 1], ss.at[q, 1], sr.at[q, 1], u_left)
        send(t_ref.at[3 * u_up + q], tiles(q, 0, sub), zs.at[q, 0], zr.at[q, 0], u_right)
        send(t_ref.at[3 * u_down + q], tiles(q, 0, sub), zs.at[q, 1], zr.at[q, 1], u_left)

    def z_relay(q):
        arrived(stage.at[q, 0], ss.at[q, 0], sr.at[q, 0])
        send(stage.at[q, 0], tiles(q, 0, u_down, 0, 2), fs.at[q, 0], fr.at[q, 0], u_right)
        arrived(stage.at[q, 1], ss.at[q, 1], sr.at[q, 1])
        send(stage.at[q, 1], tiles(q, 0, u_up, 2, 2), fs.at[q, 1], fr.at[q, 1], u_left)

    z_of = (sub, u_down, u_opp, u_up)

    def inject(q, d):
        src = tiles(q, 0, z_of[d])
        if d == 0:
            src = t_ref.at[3 * sub + q]
        elif d == 1:
            arrived(src, zs.at[q, 0], zr.at[q, 0])
        elif d == 3:
            arrived(src, zs.at[q, 1], zr.at[q, 1])
        else:
            arrived(tiles(q, 0, u_opp, 0, 2), fs.at[q, 0], fr.at[q, 0])
            arrived(tiles(q, 0, u_opp, 2, 2), fs.at[q, 1], fr.at[q, 1])
        send(src, tiles(q, 1, z_of[d]), ysr.at[q, d], yrr.at[q, d], r_right)
        send(src, tiles(q, 2, z_of[d]), ysl.at[q, d], yrl.at[q, d], r_left)

    def relay(q, d):
        zi = z_of[d]
        arrived(tiles(q, 1, zi), ysr.at[q, d], yrr.at[q, d])
        send(
            tiles(q, 1, zi, 0, 2), tiles(q, 3, zi, 0, 2), fsr.at[q, d], frr.at[q, d], r_right
        )
        arrived(tiles(q, 2, zi), ysl.at[q, d], yrl.at[q, d])
        send(
            tiles(q, 2, zi, 2, 2), tiles(q, 3, zi, 2, 2), fsl.at[q, d], frl.at[q, d], r_left
        )

    def far(q, d):
        zi = z_of[d]
        arrived(tiles(q, 3, zi, 0, 2), fsr.at[q, d], frr.at[q, d])
        arrived(tiles(q, 3, zi, 2, 2), fsl.at[q, d], frl.at[q, d])

    def o_at(zi, first=0, count=128):
        return orow.at[pl.ds(pl.multiple_of(128 * zi + first, 64), count)]

    def o_sends(h):
        right, left = 64 * h, 64 - 64 * h
        send(
            o_ref.at[pl.ds(right, 64)], o_at(sub, right, 64), hs.at[0, h], hr.at[0, h], u_right
        )
        send(o_ref.at[pl.ds(left, 64)], o_at(sub, left, 64), hs.at[1, h], hr.at[1, h], u_left)

    def o_relay():
        at = o_at(u_down, 0, 64)
        arrived(at, hs.at[0, 0], hr.at[0, 0])
        send(at, at, hfs.at[0], hfr.at[0], u_right)
        at = o_at(u_up, 64, 64)
        arrived(at, hs.at[1, 0], hr.at[1, 0])
        send(at, at, hfs.at[1], hfr.at[1], u_left)

    def o_perm(r):
        rows = pl.ds(pl.multiple_of(128 * r, 128), 128)
        for rel in range(4):
            for u in range(4):
                at = pl.multiple_of(128 * block(r_rel[rel], u), 128)
                operm[rows, pl.ds(512 * rel + 128 * u, 128)] = orow[rows, pl.ds(at, 128)]

    def o_near():
        arrived(o_at(u_down, 64, 64), hs.at[0, 1], hr.at[0, 1])
        arrived(o_at(u_up, 0, 64), hs.at[1, 1], hr.at[1, 1])
        o_perm(u_down)
        o_perm(u_up)

    def o_far():
        arrived(o_at(u_opp, 0, 64), hfs.at[0], hfr.at[0])
        arrived(o_at(u_opp, 64, 64), hfs.at[1], hfr.at[1])
        o_perm(u_opp)

    def chunk(owner, j):
        return tp.at[owner, pl.ds(3 * j, 3)]

    def x_sends(t):
        j, opp = t, (t + 2) % 4
        send(t_ref.at[pl.ds(3 * j, 3)], chunk(g, j), asr.at[j], arr.at[j], (x_right, k))
        send(t_ref.at[pl.ds(3 * opp, 3)], chunk(g, opp), asl.at[opp], arl.at[opp], (x_left, k))
        send(t_ref.at[pl.ds(3 * j, 3)], chunk(g, j), cs.at[0, j], cr.at[0, j], partner)

    def x_relay(t):
        j, opp = t, (t + 2) % 4
        at = chunk(x_left, j)
        arrived(at, asr.at[j], arr.at[j])
        if t < 2:
            send(at, at, gs.at[j], gr.at[j], (x_right, k))
        send(at, at, cs.at[1, j], cr.at[1, j], partner)
        at = chunk(x_right, opp)
        arrived(at, asl.at[opp], arl.at[opp])
        if t < 2:
            send(at, at, gs.at[opp], gr.at[opp], (x_left, k))
        send(at, at, cs.at[2, opp], cr.at[2, opp], partner)

    def x_far(t):
        for j in (t, t + 2):
            at = chunk(x_far_, j)
            arrived(at, gs.at[j], gr.at[j])
            send(at, at, cs.at[3, j], cr.at[3, j], partner)

    def x_done(j):
        for n, dx in enumerate((0, 3, 1, 2)):
            owner = ((x + dx) % 4) * 2 + 1 - core
            arrived(chunk(owner, j), cs.at[n, j], cr.at[n, j])

    def tabulate():
        for q in range(3):
            for rel in range(4):
                tqs[q][rel][16] = jnp.zeros((128, 128), BF16)
        for rel in range(4):

            def unit(u, carry):
                i = block(r_rel[rel], u)
                c0, c1, c2, c3 = (cols_ref[s, i] for s in range(4))
                n_live = live_ref[i]
                for c in range(16):
                    s = jnp.where(c1 == c, 1, jnp.where(c2 == c, 2, jnp.where(c3 == c, 3, 0)))
                    hit = (c0 == c) | (c1 == c) | (c2 == c) | (c3 == c)
                    table[64 * rel + 16 * u + c] = jnp.where(hit & (s < n_live), 4 * u + s, 16)
                return carry

            lax.fori_loop(0, 4, unit, 0)

    def fill_unit(q, rel, u):
        dst = (big0, big1, big0)[q]
        at = pl.multiple_of(512 * rel + 128 * u, 128)
        for c in range(16):
            tile = tqs[q][rel][table[64 * rel + 16 * u + c]]
            dst[pl.ds(at, 128), pl.ds(128 * c, 128)] = tile

    def fill_rel(q, rel):
        def unit(u, carry):
            fill_unit(q, rel, u)
            return carry

        lax.fori_loop(0, 4, unit, 0)

    def rows_product(blocks):
        for c in range(0, 2048, 256):
            for r in blocks:
                rows = pl.ds(pl.multiple_of(128 * r, 128), 128)
                acc = jnp.dot(
                    operm[rows, :], big0[:, pl.ds(c, 256)], preferred_element_type=F32
                )
                nn[rows, pl.ds(c, 256)] = acc.astype(BF16)

    def early_product(q, fills):
        big = (big0, big1, big0)[q]
        for n in range(8):
            c = 256 * n
            nacc[:, pl.ds(c, 256)] = jnp.dot(
                operm[:, pl.ds(0, 1536)], big[pl.ds(0, 1536), pl.ds(c, 256)],
                preferred_element_type=F32,
            )
            if n % 2 == 0 and n // 2 < len(fills):
                fill_unit(*fills[n // 2])

    def late_product(q):
        big = (big0, big1, big0)[q]
        for c in range(0, 2048, 256):
            acc = nacc[:, pl.ds(c, 256)] + jnp.dot(
                operm[:, pl.ds(1536, 512)], big[pl.ds(1536, 512), pl.ds(c, 256)],
                preferred_element_type=F32,
            )
            nn[:, pl.ds(c, 256)] = acc.astype(BF16)

    def x_rows(r, dst, first):
        lhs = nn[pl.ds(pl.multiple_of(128 * r, 128), 128), :]
        i = block(ring, r)
        rhs = jnp.concatenate([vv[cols_ref[first + e, i]] for e in range(2)], axis=1)
        acc = jnp.dot(lhs, rhs, preferred_element_type=F32)
        for e in range(2):
            tile = acc[:, 128 * e : 128 * e + 128]
            dst[first + e] = jnp.where(first + e < live_ref[i], tile, 0.0).astype(BF16)

    def piece(m):
        q = min(m, 2)
        first, count = (0, 4) if m < 2 else (2 * m - 4, 2)
        return q, first, first + count // 2, count // 2

    def e_opp(m):
        q, a, b, n = piece(m)
        src = xs.at[q, u_opp]
        if m >= 1:
            at = pl.ds(a, 2 * n)
            send(src.at[at], xr.at[q, sub, at], us.at[m, 0], ur.at[m, 0], u_across)
            return
        lo, hi = xstage.at[m, 0, pl.ds(0, n)], xstage.at[m, 1, pl.ds(0, n)]
        send(src.at[pl.ds(a, n)], lo, us.at[m, 0], ur.at[m, 0], u_right)
        send(src.at[pl.ds(b, n)], hi, us.at[m, 1], ur.at[m, 1], u_left)

    def e_up(m):
        q, a, b, n = piece(m)
        at = pl.ds(a, 2 * n)
        send(xs.at[q, u_up, at], xr.at[q, sub, at], es.at[m, 0], er.at[m, 0], u_right)

    def e_down(m):
        q, a, b, n = piece(m)
        at = pl.ds(a, 2 * n)
        send(xs.at[q, u_down, at], xr.at[q, sub, at], es.at[m, 1], er.at[m, 1], u_left)

    def e_relay(m):
        q, a, b, n = piece(m)
        at = xstage.at[m, 0, pl.ds(0, n)]
        arrived(at, us.at[m, 0], ur.at[m, 0])
        send(at, xr.at[q, u_down, pl.ds(a, n)], ws.at[m, 0], wr.at[m, 0], u_right)
        at = xstage.at[m, 1, pl.ds(0, n)]
        arrived(at, us.at[m, 1], ur.at[m, 1])
        send(at, xr.at[q, u_up, pl.ds(b, n)], ws.at[m, 1], wr.at[m, 1], u_left)

    def e_done(m):
        q, a, b, n = piece(m)
        at = pl.ds(a, 2 * n)
        arrived(xr.at[q, u_down, at], es.at[m, 0], er.at[m, 0])
        arrived(xr.at[q, u_up, at], es.at[m, 1], er.at[m, 1])
        if m >= 1:
            arrived(xr.at[q, u_opp, at], us.at[m, 0], ur.at[m, 0])
            return
        arrived(xr.at[q, u_opp, pl.ds(a, n)], ws.at[m, 0], wr.at[m, 0])
        arrived(xr.at[q, u_opp, pl.ds(b, n)], ws.at[m, 1], wr.at[m, 1])

    def x_part(m, fills=()):
        q, a, b, n = piece(m)
        todo = list(fills)
        for r in (u_opp, u_up, u_down, sub):
            dst = xr.at[q, sub] if r is sub else xs.at[q, r]
            for first in (0, 2) if n == 2 else (a,):
                x_rows(r, dst, first)
                if todo:
                    fill_unit(*todo.pop(0))
        e_opp(m)
        e_up(m)
        e_down(m)

    def contract(h):
        def body(n, carry):
            lhs, rhs = [], []
            for e in range(4):
                a = pl.multiple_of(64 * n + 16 * e, 16)
                for s in (2 * h, 2 * h + 1):
                    lhs.append(tp[:, :, s, pl.ds(a, 16), :].reshape(1536, 128))
                    rhs.append(xr[:, :, s, pl.ds(a, 16), :].reshape(192, 128))
            cacc[...] += lax.dot_general(
                jnp.concatenate(lhs, axis=1), jnp.concatenate(rhs, axis=1),
                (((1,), (1,)), ((), ())), preferred_element_type=F32,
            )
            return carry

        lax.fori_loop(0, 2, body, 0)

    z_sends(0)
    inject(0, 0)
    x_sends(0)
    inject(1, 0)
    inject(2, 0)
    z_relay(0)
    inject(0, 1)
    inject(0, 3)
    z_sends(1)
    inject(0, 2)
    relay(0, 0)
    x_sends(1)
    x_sends(2)
    x_sends(3)
    for copy in t_local + v_local:
        copy.wait()
    o_local.wait()
    o_perm(sub)
    o_sends(0)
    z_relay(1)
    o_sends(1)
    tabulate()
    relay(0, 1)
    relay(0, 3)
    o_relay()
    z_sends(2)
    fill_rel(0, 0)
    relay(0, 2)
    relay(1, 0)
    x_relay(0)
    inject(1, 1)
    inject(1, 3)
    fill_rel(0, 1)
    inject(1, 2)
    relay(2, 0)
    fill_rel(0, 2)
    x_relay(1)
    for d in range(4):
        far(0, d)
    fill_rel(0, 3)
    rows_product([sub])
    fill_rel(1, 0)
    relay(1, 1)
    o_near()
    rows_product([u_down, u_up])
    relay(1, 3)
    z_relay(2)
    x_relay(2)
    o_far()
    rows_product([u_opp])
    relay(1, 2)
    x_part(0, [(1, 1, u) for u in range(4)] + [(1, 2, u) for u in range(4)])
    inject(2, 1)
    inject(2, 3)
    inject(2, 2)
    early_product(1, [(2, 0, u) for u in range(4)])
    relay(2, 1)
    for d in range(4):
        far(1, d)
    fill_rel(1, 3)
    late_product(1)
    relay(2, 3)
    x_relay(3)
    e_relay(0)
    relay(2, 2)
    x_part(1, [(2, 1, u) for u in range(4)] + [(2, 2, u) for u in range(4)])
    early_product(2, [])
    x_far(0)
    for d in range(4):
        far(2, d)
    fill_rel(2, 3)
    late_product(2)
    x_part(2)
    x_part(3)
    x_far(1)
    cacc[...] = jnp.zeros_like(cacc)
    dsum[...] = jnp.zeros_like(dsum)
    part[...] = jnp.zeros_like(part)
    e_done(0)
    e_done(1)
    e_done(2)
    for j in range(4):
        x_done(j)
    p_local.wait()
    contract(0)
    e_done(3)
    contract(1)
    row = lax.broadcasted_iota(jnp.int32, (192, 192), 0)
    col = lax.broadcasted_iota(jnp.int32, (192, 192), 1)
    same = (row % 16) == (col % 16)
    row = lax.broadcasted_iota(jnp.int32, (192, 128), 0)
    col = lax.broadcasted_iota(jnp.int32, (192, 128), 1)
    pick = (3 * (row // 16 % 4) + row // 64 == col).astype(F32)
    for owner in range(8):
        kept = jnp.where(same, cacc[pl.ds(192 * owner, 192), :], 0.0)
        dsum[owner, pl.ds(0, 12), :] = jnp.sum(kept.reshape(12, 16, 192), axis=1)
    summed = jnp.dot(
        dsum[...].reshape(128, 192), pick,
        preferred_element_type=F32, precision=lax.Precision.HIGHEST,
    ).reshape(8, 16, 128)
    for owner in range(8):
        part[2 * owner, pl.ds(0, 6), :] = summed[owner, :6]
        part[2 * owner + 1, pl.ds(0, 6), :] = summed[owner, 6:12]

    for d in range(1, 16):
        to = (k + d) % 16
        send(part.at[to], red.at[d], rs.at[d], rr.at[d], (g, to))
    total = part[k]
    for d in range(1, 16):
        arrived(red.at[d], rs.at[d], rr.at[d])
        total += red[d]
    out_ref[...] = total[:6, :12]
    for copy in started:
        copy.wait_send()


def per_device(three_centre, occ_green, virt_green, tile_cols, tile_live):
    factor = 1.0 / (128 * math.sqrt(64))
    any_space = pl.BlockSpec(memory_space=pl.ANY)
    smem = pl.BlockSpec(memory_space=pltpu.SMEM)
    dma = pltpu.SemaphoreType.DMA
    chi = pl.pallas_call(
        kernel,
        out_shape=jax.ShapeDtypeStruct((6, 12), F32),
        in_specs=[smem, smem, any_space, any_space, any_space],
        out_specs=pl.BlockSpec(memory_space=pltpu.VMEM),
        scratch_shapes=[pltpu.VMEM((17, 128, 128), BF16)] * 12
        + [
            pltpu.VMEM((512, 2048), BF16),
            pltpu.VMEM((512, 2048), BF16),
            pltpu.VMEM((16, 2048, 128), BF16),
            pltpu.VMEM((8, 12, 4, 128, 128), BF16),
            pltpu.VMEM((512, 2048), BF16),
            pltpu.VMEM((512, 2048), F32),
            pltpu.VMEM((2048, 2048), BF16),
            pltpu.VMEM((2048, 2048), BF16),
            pltpu.VMEM((3, 2, 2, 128, 128), BF16),
            pltpu.VMEM((4, 2, 2, 128, 128), BF16),
            pltpu.VMEM((3, 4, 4, 128, 128), BF16),
            pltpu.VMEM((3, 4, 4, 128, 128), BF16),
            pltpu.VMEM((1536, 192), F32),
            pltpu.VMEM((8, 16, 192), F32),
            pltpu.VMEM((16, 8, 128), F32),
            pltpu.VMEM((16, 8, 128), F32),
            pltpu.SMEM((256,), jnp.int32),
            dma((21,)),
            dma((3, 2)), dma((3, 2)), dma((3, 2)), dma((3, 2)), dma((3, 2)), dma((3, 2)),
            dma((2, 2)), dma((2, 2)), dma((2,)), dma((2,)),
            dma((3, 4)), dma((3, 4)), dma((3, 4)), dma((3, 4)),
            dma((3, 4)), dma((3, 4)), dma((3, 4)), dma((3, 4)),
            dma((4,)), dma((4,)), dma((4,)), dma((4,)), dma((4,)), dma((4,)),
            dma((4, 4)), dma((4, 4)),
            dma((4, 2)), dma((4, 2)), dma((4, 2)), dma((4, 2)), dma((4, 2)), dma((4, 2)),
            dma((16,)), dma((16,)),
        ],
        compiler_params=pltpu.CompilerParams(
            collective_id=0, has_side_effects=True, vmem_limit_bytes=67043328
        ),
    )(tile_cols.T, tile_live, three_centre, occ_green, virt_green)
    return chi * factor


def solution(mesh):
    placed = (P("aux", "pair", None, None), P("pair", None), P(), P(), P())
    return jax.shard_map(
        per_device, mesh=mesh, in_specs=placed, out_specs=P("pair", "aux"), check_vma=False
    )
```

```python
import math

import jax
import jax.numpy as jnp
from jax import lax
from jax.experimental import pallas as pl
from jax.experimental.pallas import tpu as pltpu
from jax.sharding import PartitionSpec as P

MESH = pl.DeviceIdType.MESH
F32 = jnp.float32
BF16 = jnp.bfloat16


def kernel(
    cols_ref, live_ref, t_ref, o_ref, v_ref, out_ref,
    tq00, tq01, tq02, tq03, tq10, tq11, tq12, tq13, tq20, tq21, tq22, tq23,
    orow, operm, vv, tp, nn, nacc, big0, big1, stage, xstage, xs, xr, cacc, dsum, part, red, table,
    loc, zs, zr, ss, sr, fs, fr, hs, hr, hfs, hfr,
    ysr, yrr, ysl, yrl, fsr, frr, fsl, frl,
    asr, arr, asl, arl, gs, gr, cs, cr, es, er, us, ur, ws, wr, rs, rr,
):
    tqs = ((tq00, tq01, tq02, tq03), (tq10, tq11, tq12, tq13), (tq20, tq21, tq22, tq23))
    g = lax.axis_index("aux")
    k = lax.axis_index("pair")
    y, z = k // 4, k % 4
    x, core = g // 2, g % 2
    partner = (x * 2 + 1 - core, k)
    x_right, x_left, x_far_ = (
        ((x + 1) % 4) * 2 + core, ((x + 3) % 4) * 2 + core, ((x + 2) % 4) * 2 + core,
    )
    ring, sub = y + core * (z - y), z + core * (y - z)
    ring_step, sub_step = 4 - 3 * core, 1 + 3 * core

    def block(r, u):
        return r * ring_step + u * sub_step

    r_rel = (ring, (ring + 3) % 4, (ring + 1) % 4, (ring + 2) % 4)
    r_right, r_left = (g, block(r_rel[2], sub)), (g, block(r_rel[1], sub))
    u_up, u_down, u_opp = (sub + 1) % 4, (sub + 3) % 4, (sub + 2) % 4
    u_right, u_left = (g, block(ring, u_up)), (g, block(ring, u_down))
    u_across = (g, block(ring, u_opp))

    barrier = pltpu.get_barrier_semaphore()
    peers = [r_right, r_left, u_right, u_left, (x_right, k), (x_left, k), partner]
    for peer in peers:
        pl.semaphore_signal(barrier, inc=1, device_id=peer, device_id_type=MESH)

    started = []

    def local(src, dst, sem):
        copy = pltpu.make_async_copy(src, dst, sem)
        copy.start()
        return copy

    def send(src, dst, send_sem, recv_sem, device):
        copy = pltpu.make_async_remote_copy(
            src_ref=src, dst_ref=dst, send_sem=send_sem, recv_sem=recv_sem,
            device_id=device, device_id_type=MESH,
        )
        copy.start()
        started.append(copy)

    def arrived(dst, send_sem, recv_sem):
        pltpu.make_async_remote_copy(
            src_ref=dst, dst_ref=dst, send_sem=send_sem, recv_sem=recv_sem,
            device_id=partner, device_id_type=MESH,
        ).wait_recv()

    def tiles(q, rel, zi, first=0, count=4):
        return tqs[q][rel].at[pl.ds(4 * zi + first, count)]

    t_local = [local(t_ref.at[3 * sub + q], tiles(q, 0, sub), loc.at[q]) for q in range(3)]
    o_local = local(o_ref, orow.at[pl.ds(pl.multiple_of(128 * sub, 128), 128)], loc.at[4])
    v_local = [
        local(v_ref.at[:, pl.ds(128 * c, 128)], vv.at[c], loc.at[5 + c]) for c in range(16)
    ]
    p_local = local(t_ref, tp.at[g], loc.at[3])
    pl.semaphore_wait(barrier, len(peers))

    def z_sends(q):
        opp = 3 * u_opp + q
        send(
            t_ref.at[opp, pl.ds(0, 2)], stage.at[q, 0], ss.at[q, 0], sr.at[q, 0], u_right
        )
        send(t_ref.at[opp, pl.ds(2, 2)], stage.at[q, 1], ss.at[q, 1], sr.at[q, 1], u_left)
        send(t_ref.at[3 * u_up + q], tiles(q, 0, sub), zs.at[q, 0], zr.at[q, 0], u_right)
        send(t_ref.at[3 * u_down + q], tiles(q, 0, sub), zs.at[q, 1], zr.at[q, 1], u_left)

    def z_relay(q):
        arrived(stage.at[q, 0], ss.at[q, 0], sr.at[q, 0])
        send(stage.at[q, 0], tiles(q, 0, u_down, 0, 2), fs.at[q, 0], fr.at[q, 0], u_right)
        arrived(stage.at[q, 1], ss.at[q, 1], sr.at[q, 1])
        send(stage.at[q, 1], tiles(q, 0, u_up, 2, 2), fs.at[q, 1], fr.at[q, 1], u_left)

    z_of = (sub, u_down, u_opp, u_up)

    def inject(q, d):
        src = tiles(q, 0, z_of[d])
        if d == 0:
            src = t_ref.at[3 * sub + q]
        elif d == 1:
            arrived(src, zs.at[q, 0], zr.at[q, 0])
        elif d == 3:
            arrived(src, zs.at[q, 1], zr.at[q, 1])
        else:
            arrived(tiles(q, 0, u_opp, 0, 2), fs.at[q, 0], fr.at[q, 0])
            arrived(tiles(q, 0, u_opp, 2, 2), fs.at[q, 1], fr.at[q, 1])
        send(src, tiles(q, 1, z_of[d]), ysr.at[q, d], yrr.at[q, d], r_right)
        send(src, tiles(q, 2, z_of[d]), ysl.at[q, d], yrl.at[q, d], r_left)

    def relay(q, d):
        zi = z_of[d]
        arrived(tiles(q, 1, zi), ysr.at[q, d], yrr.at[q, d])
        send(
            tiles(q, 1, zi, 0, 2), tiles(q, 3, zi, 0, 2), fsr.at[q, d], frr.at[q, d], r_right
        )
        arrived(tiles(q, 2, zi), ysl.at[q, d], yrl.at[q, d])
        send(
            tiles(q, 2, zi, 2, 2), tiles(q, 3, zi, 2, 2), fsl.at[q, d], frl.at[q, d], r_left
        )

    def far(q, d):
        zi = z_of[d]
        arrived(tiles(q, 3, zi, 0, 2), fsr.at[q, d], frr.at[q, d])
        arrived(tiles(q, 3, zi, 2, 2), fsl.at[q, d], frl.at[q, d])

    def o_at(zi, first=0, count=128):
        return orow.at[pl.ds(pl.multiple_of(128 * zi + first, 64), count)]

    def o_sends(h):
        right, left = 64 * h, 64 - 64 * h
        send(
            o_ref.at[pl.ds(right, 64)], o_at(sub, right, 64), hs.at[0, h], hr.at[0, h], u_right
        )
        send(o_ref.at[pl.ds(left, 64)], o_at(sub, left, 64), hs.at[1, h], hr.at[1, h], u_left)

    def o_relay():
        at = o_at(u_down, 0, 64)
        arrived(at, hs.at[0, 0], hr.at[0, 0])
        send(at, at, hfs.at[0], hfr.at[0], u_right)
        at = o_at(u_up, 64, 64)
        arrived(at, hs.at[1, 0], hr.at[1, 0])
        send(at, at, hfs.at[1], hfr.at[1], u_left)

    def o_perm(r):
        rows = pl.ds(pl.multiple_of(128 * r, 128), 128)
        for rel in range(4):
            for u in range(4):
                at = pl.multiple_of(128 * block(r_rel[rel], u), 128)
                operm[rows, pl.ds(512 * rel + 128 * u, 128)] = orow[rows, pl.ds(at, 128)]

    def o_near():
        arrived(o_at(u_down, 64, 64), hs.at[0, 1], hr.at[0, 1])
        arrived(o_at(u_up, 0, 64), hs.at[1, 1], hr.at[1, 1])
        o_perm(u_down)
        o_perm(u_up)

    def o_far():
        arrived(o_at(u_opp, 0, 64), hfs.at[0], hfr.at[0])
        arrived(o_at(u_opp, 64, 64), hfs.at[1], hfr.at[1])
        o_perm(u_opp)

    def chunk(owner, j):
        return tp.at[owner, pl.ds(3 * j, 3)]

    def x_sends(t):
        j, opp = t, (t + 2) % 4
        send(t_ref.at[pl.ds(3 * j, 3)], chunk(g, j), asr.at[j], arr.at[j], (x_right, k))
        send(t_ref.at[pl.ds(3 * opp, 3)], chunk(g, opp), asl.at[opp], arl.at[opp], (x_left, k))
        send(t_ref.at[pl.ds(3 * j, 3)], chunk(g, j), cs.at[0, j], cr.at[0, j], partner)

    def x_relay(t):
        j, opp = t, (t + 2) % 4
        at = chunk(x_left, j)
        arrived(at, asr.at[j], arr.at[j])
        if t < 2:
            send(at, at, gs.at[j], gr.at[j], (x_right, k))
        send(at, at, cs.at[1, j], cr.at[1, j], partner)
        at = chunk(x_right, opp)
        arrived(at, asl.at[opp], arl.at[opp])
        if t < 2:
            send(at, at, gs.at[opp], gr.at[opp], (x_left, k))
        send(at, at, cs.at[2, opp], cr.at[2, opp], partner)

    def x_far(t):
        for j in (t, t + 2):
            at = chunk(x_far_, j)
            arrived(at, gs.at[j], gr.at[j])
            send(at, at, cs.at[3, j], cr.at[3, j], partner)

    def x_done(j):
        for n, dx in enumerate((0, 3, 1, 2)):
            owner = ((x + dx) % 4) * 2 + 1 - core
            arrived(chunk(owner, j), cs.at[n, j], cr.at[n, j])

    def tabulate():
        for q in range(3):
            for rel in range(4):
                tqs[q][rel][16] = jnp.zeros((128, 128), BF16)
        for rel in range(4):

            def unit(u, carry):
                i = block(r_rel[rel], u)
                c0, c1, c2, c3 = (cols_ref[s, i] for s in range(4))
                n_live = live_ref[i]
                for c in range(16):
                    s = jnp.where(c1 == c, 1, jnp.where(c2 == c, 2, jnp.where(c3 == c, 3, 0)))
                    hit = (c0 == c) | (c1 == c) | (c2 == c) | (c3 == c)
                    table[64 * rel + 16 * u + c] = jnp.where(hit & (s < n_live), 4 * u + s, 16)
                return carry

            lax.fori_loop(0, 4, unit, 0)

    def fill_unit(q, rel, u):
        dst = (big0, big1, big0)[q]
        at = pl.multiple_of(512 * rel + 128 * u, 128)
        for c in range(16):
            tile = tqs[q][rel][table[64 * rel + 16 * u + c]]
            dst[pl.ds(at, 128), pl.ds(128 * c, 128)] = tile

    def fill_rel(q, rel):
        def unit(u, carry):
            fill_unit(q, rel, u)
            return carry

        lax.fori_loop(0, 4, unit, 0)

    def rows_product(blocks):
        for c in range(0, 2048, 256):
            for r in blocks:
                rows = pl.ds(pl.multiple_of(128 * r, 128), 128)
                acc = jnp.dot(
                    operm[rows, :], big0[:, pl.ds(c, 256)], preferred_element_type=F32
                )
                nn[rows, pl.ds(c, 256)] = acc.astype(BF16)

    def product(q, rel, count, fills=()):
        big = (big0, big1, big0)[q]
        span = pl.ds(512 * rel, 512 * count)
        for n in range(8):
            at = pl.ds(256 * n, 256)
            acc = jnp.dot(operm[:, span], big[span, at], preferred_element_type=F32)
            if rel:
                acc += nacc[:, at]
            if rel + count == 4:
                nn[:, at] = acc.astype(BF16)
            else:
                nacc[:, at] = acc
            if n % 2 == 0 and n // 2 < len(fills):
                fill_unit(*fills[n // 2])

    def x_rows(r, dst, first):
        lhs = nn[pl.ds(pl.multiple_of(128 * r, 128), 128), :]
        i = block(ring, r)
        rhs = jnp.concatenate([vv[cols_ref[first + e, i]] for e in range(2)], axis=1)
        acc = jnp.dot(lhs, rhs, preferred_element_type=F32)
        for e in range(2):
            tile = acc[:, 128 * e : 128 * e + 128]
            dst[first + e] = jnp.where(first + e < live_ref[i], tile, 0.0).astype(BF16)

    def piece(m):
        q = min(m, 2)
        first, count = (0, 4) if m < 2 else (2 * m - 4, 2)
        return q, first, first + count // 2, count // 2

    def e_opp(m):
        q, a, b, n = piece(m)
        src = xs.at[q, u_opp]
        if m >= 2:
            at = pl.ds(a, 2 * n)
            send(src.at[at], xr.at[q, sub, at], us.at[m, 0], ur.at[m, 0], u_across)
            return
        lo, hi = xstage.at[m, 0, pl.ds(0, n)], xstage.at[m, 1, pl.ds(0, n)]
        send(src.at[pl.ds(a, n)], lo, us.at[m, 0], ur.at[m, 0], u_right)
        send(src.at[pl.ds(b, n)], hi, us.at[m, 1], ur.at[m, 1], u_left)

    def e_up(m):
        q, a, b, n = piece(m)
        at = pl.ds(a, 2 * n)
        send(xs.at[q, u_up, at], xr.at[q, sub, at], es.at[m, 0], er.at[m, 0], u_right)

    def e_down(m):
        q, a, b, n = piece(m)
        at = pl.ds(a, 2 * n)
        send(xs.at[q, u_down, at], xr.at[q, sub, at], es.at[m, 1], er.at[m, 1], u_left)

    def e_relay(m):
        q, a, b, n = piece(m)
        at = xstage.at[m, 0, pl.ds(0, n)]
        arrived(at, us.at[m, 0], ur.at[m, 0])
        send(at, xr.at[q, u_down, pl.ds(a, n)], ws.at[m, 0], wr.at[m, 0], u_right)
        at = xstage.at[m, 1, pl.ds(0, n)]
        arrived(at, us.at[m, 1], ur.at[m, 1])
        send(at, xr.at[q, u_up, pl.ds(b, n)], ws.at[m, 1], wr.at[m, 1], u_left)

    def e_done(m):
        q, a, b, n = piece(m)
        at = pl.ds(a, 2 * n)
        arrived(xr.at[q, u_down, at], es.at[m, 0], er.at[m, 0])
        arrived(xr.at[q, u_up, at], es.at[m, 1], er.at[m, 1])
        if m >= 2:
            arrived(xr.at[q, u_opp, at], us.at[m, 0], ur.at[m, 0])
            return
        arrived(xr.at[q, u_opp, pl.ds(a, n)], ws.at[m, 0], wr.at[m, 0])
        arrived(xr.at[q, u_opp, pl.ds(b, n)], ws.at[m, 1], wr.at[m, 1])

    def e_send(m):
        e_opp(m)
        e_up(m)
        e_down(m)

    def x_part(m, fills=(), between=None):
        q, a, b, n = piece(m)
        todo = list(fills)
        for r in (u_opp, u_up, u_down, sub):
            dst = xr.at[q, sub] if r is sub else xs.at[q, r]
            for first in (0, 2) if n == 2 else (a,):
                x_rows(r, dst, first)
                if todo:
                    fill_unit(*todo.pop(0))
            if r is u_up and between is not None:
                between()

    def contract(h):
        def body(n, carry):
            lhs, rhs = [], []
            for e in range(4):
                a = pl.multiple_of(64 * n + 16 * e, 16)
                for s in (2 * h, 2 * h + 1):
                    lhs.append(tp[:, :, s, pl.ds(a, 16), :].reshape(1536, 128))
                    rhs.append(xr[:, :, s, pl.ds(a, 16), :].reshape(192, 128))
            cacc[...] += lax.dot_general(
                jnp.concatenate(lhs, axis=1), jnp.concatenate(rhs, axis=1),
                (((1,), (1,)), ((), ())), preferred_element_type=F32,
            )
            return carry

        lax.fori_loop(0, 2, body, 0)

    def inject_near():
        inject(2, 1)
        inject(2, 3)

    z_sends(0)
    inject(0, 0)
    x_sends(0)
    inject(1, 0)
    inject(2, 0)
    z_relay(0)
    inject(0, 1)
    inject(0, 3)
    z_sends(1)
    inject(0, 2)
    relay(0, 0)
    x_sends(1)
    x_sends(2)
    x_sends(3)
    for copy in t_local + v_local:
        copy.wait()
    o_local.wait()
    o_perm(sub)
    o_sends(0)
    z_relay(1)
    o_sends(1)
    tabulate()
    relay(0, 1)
    relay(0, 3)
    o_relay()
    z_sends(2)
    fill_rel(0, 0)
    relay(0, 2)
    relay(1, 0)
    x_relay(0)
    inject(1, 1)
    inject(1, 3)
    fill_rel(0, 1)
    inject(1, 2)
    relay(2, 0)
    fill_rel(0, 2)
    x_relay(1)
    for d in range(4):
        far(0, d)
    fill_rel(0, 3)
    rows_product([sub])
    fill_rel(1, 0)
    relay(1, 1)
    o_near()
    rows_product([u_down, u_up])
    relay(1, 3)
    z_relay(2)
    x_relay(2)
    o_far()
    rows_product([u_opp])
    relay(1, 2)
    x_part(0, [(1, 1, u) for u in range(4)] + [(1, 2, u) for u in range(4)], inject_near)
    inject(2, 2)
    product(1, 0, 3, [(2, 0, u) for u in range(4)])
    for d in range(4):
        far(1, d)
    fill_rel(1, 3)
    relay(2, 1)
    product(1, 3, 1)
    relay(2, 3)
    x_relay(3)
    x_part(1)
    relay(2, 2)
    e_send(0)
    e_send(1)
    product(2, 0, 1)
    fill_rel(2, 1)
    fill_rel(2, 2)
    product(2, 1, 2)
    x_far(0)
    for d in range(4):
        far(2, d)
    fill_rel(2, 3)
    e_relay(0)
    product(2, 3, 1)
    e_relay(1)
    x_part(2)
    e_send(2)
    x_part(3)
    e_send(3)
    x_far(1)
    cacc[...] = jnp.zeros_like(cacc)
    dsum[...] = jnp.zeros_like(dsum)
    part[...] = jnp.zeros_like(part)
    e_done(0)
    e_done(1)
    e_done(2)
    for j in range(4):
        x_done(j)
    p_local.wait()
    contract(0)
    e_done(3)
    contract(1)
    row = lax.broadcasted_iota(jnp.int32, (192, 192), 0)
    col = lax.broadcasted_iota(jnp.int32, (192, 192), 1)
    same = (row % 16) == (col % 16)
    row = lax.broadcasted_iota(jnp.int32, (192, 128), 0)
    col = lax.broadcasted_iota(jnp.int32, (192, 128), 1)
    pick = (3 * (row // 16 % 4) + row // 64 == col).astype(F32)
    for owner in range(8):
        kept = jnp.where(same, cacc[pl.ds(192 * owner, 192), :], 0.0)
        dsum[owner, pl.ds(0, 12), :] = jnp.sum(kept.reshape(12, 16, 192), axis=1)
    summed = jnp.dot(
        dsum[...].reshape(128, 192), pick,
        preferred_element_type=F32, precision=lax.Precision.HIGHEST,
    ).reshape(8, 16, 128)
    for owner in range(8):
        part[2 * owner, pl.ds(0, 6), :] = summed[owner, :6]
        part[2 * owner + 1, pl.ds(0, 6), :] = summed[owner, 6:12]

    for d in range(1, 16):
        to = (k + d) % 16
        send(part.at[to], red.at[d], rs.at[d], rr.at[d], (g, to))
    total = part[k]
    for d in range(1, 16):
        arrived(red.at[d], rs.at[d], rr.at[d])
        total += red[d]
    out_ref[...] = total[:6, :12]
    for copy in started:
        copy.wait_send()


def per_device(three_centre, occ_green, virt_green, tile_cols, tile_live):
    factor = 1.0 / (128 * math.sqrt(64))
    any_space = pl.BlockSpec(memory_space=pl.ANY)
    smem = pl.BlockSpec(memory_space=pltpu.SMEM)
    dma = pltpu.SemaphoreType.DMA
    chi = pl.pallas_call(
        kernel,
        out_shape=jax.ShapeDtypeStruct((6, 12), F32),
        in_specs=[smem, smem, any_space, any_space, any_space],
        out_specs=pl.BlockSpec(memory_space=pltpu.VMEM),
        scratch_shapes=[pltpu.VMEM((17, 128, 128), BF16)] * 12
        + [
            pltpu.VMEM((512, 2048), BF16),
            pltpu.VMEM((512, 2048), BF16),
            pltpu.VMEM((16, 2048, 128), BF16),
            pltpu.VMEM((8, 12, 4, 128, 128), BF16),
            pltpu.VMEM((512, 2048), BF16),
            pltpu.VMEM((512, 2048), F32),
            pltpu.VMEM((2048, 2048), BF16),
            pltpu.VMEM((2048, 2048), BF16),
            pltpu.VMEM((3, 2, 2, 128, 128), BF16),
            pltpu.VMEM((4, 2, 2, 128, 128), BF16),
            pltpu.VMEM((3, 4, 4, 128, 128), BF16),
            pltpu.VMEM((3, 4, 4, 128, 128), BF16),
            pltpu.VMEM((1536, 192), F32),
            pltpu.VMEM((8, 16, 192), F32),
            pltpu.VMEM((16, 8, 128), F32),
            pltpu.VMEM((16, 8, 128), F32),
            pltpu.SMEM((256,), jnp.int32),
            dma((21,)),
            dma((3, 2)), dma((3, 2)), dma((3, 2)), dma((3, 2)), dma((3, 2)), dma((3, 2)),
            dma((2, 2)), dma((2, 2)), dma((2,)), dma((2,)),
            dma((3, 4)), dma((3, 4)), dma((3, 4)), dma((3, 4)),
            dma((3, 4)), dma((3, 4)), dma((3, 4)), dma((3, 4)),
            dma((4,)), dma((4,)), dma((4,)), dma((4,)), dma((4,)), dma((4,)),
            dma((4, 4)), dma((4, 4)),
            dma((4, 2)), dma((4, 2)), dma((4, 2)), dma((4, 2)), dma((4, 2)), dma((4, 2)),
            dma((16,)), dma((16,)),
        ],
        compiler_params=pltpu.CompilerParams(
            collective_id=0, has_side_effects=True, vmem_limit_bytes=67043328
        ),
    )(tile_cols.T, tile_live, three_centre, occ_green, virt_green)
    return chi * factor


def solution(mesh):
    placed = (P("aux", "pair", None, None), P("pair", None), P(), P(), P())
    return jax.shard_map(
        per_device, mesh=mesh, in_specs=placed, out_specs=P("pair", "aux"), check_vma=False
    )
```
